32 devices in a mesh: stn: 4 (over z), chan: 8 (over y, x, core).
Axes of the slice: x: 2, y: 2, z: 4, core: 2. Of those that a mesh axis runs over, the one named last changes fastest.
Arguments:
- voltages: bfloat16 [1024, 8, 8, 1024], P('stn', 'chan'), may hold values from -6 to 6
- fir_taps: float32 [8, 8, 1024], replicated, may hold values from -2.5 to 2.5
Outputs:
- visibilities: float32 [4, 64, 2, 1024, 1024], P(None, 'chan', None, 'stn')
The draws below stay inside these ranges and needn't reach their ends.
All inputs are finite; a program needn't handle non-finite values.
Results may differ from the reference program's by a relative error of at most 0.0044.
Values may be sent and summed in bfloat16 or wider, within the bound.
No kernel may reach another device: no remote copies, remote signals or barrier semaphores. Data moves between devices by JAX's collectives and lax.ppermute only.
A program may use at most 192 MiB of HBM per device.

```python
import math
import jax
import jax.numpy as jnp
from jax import lax

INPUTS = 1024
SLOTS = 1024
PHASES = 8
TAPS = 8
AVG = 16
FR_DEV = 8
GROUPS = 1


def steps_of(key, dims, shards, smallest, high):
    def one(position, shards_of):
        draws = jax.random.uniform(jax.random.fold_in(jax.random.fold_in(key, 6), position), (shards_of,), jnp.float32, smallest / len(shards), high / len(shards))
        return jnp.repeat(jnp.exp(draws), dims[position] // shards_of).reshape((-1,) + (1,) * (len(dims) - position - 1))

    level = one(*shards[0])
    for cut in shards[1:]:
        level = level * one(*cut)
    return level


def scatter_about(own_key, extent, deviation, bound, cuts=(), held_as=jnp.bfloat16):
    array = deviation * jax.random.normal(own_key, extent, jnp.float32)
    if cuts:
        array = array * steps_of(own_key, extent, cuts, -0.22, 0.18)
    return jnp.clip(array, -bound, bound).astype(held_as)


def setup_inputs(seed: int = 0) -> dict:
    arg_keys = jax.random.split(jax.random.key(seed), 3)
    voltages = scatter_about(arg_keys[0], (INPUTS, GROUPS * PHASES, FR_DEV, SLOTS), 1.0, 6.0, ((0, 4), (1, 8)))
    fir_taps = scatter_about(arg_keys[1], (PHASES, TAPS, SLOTS), 0.35, 2.5, (), jnp.float32)
    return {"voltages": voltages, "fir_taps": fir_taps}


def reference(voltages, fir_taps):
    inputs = voltages.shape[0]
    groups = voltages.shape[1] // PHASES
    frames = groups * FR_DEV
    spectra_count = frames - (TAPS - 1)
    band_count = PHASES // 2
    frame_len = PHASES * SLOTS
    ordered = voltages.reshape(inputs, groups, PHASES, FR_DEV, SLOTS)
    ordered = ordered.transpose(0, 1, 3, 2, 4).reshape(inputs, frames, PHASES, SLOTS)
    phase_ids = jnp.arange(PHASES, dtype=jnp.int32)
    slot_ids = jnp.arange(SLOTS, dtype=jnp.int32)
    turn_ids = (phase_ids[:, None] * slot_ids[None, :]) % frame_len
    angles = turn_ids.astype(jnp.float32) * jnp.float32(-2.0 * math.pi / frame_len)
    twist_re = jnp.cos(angles)
    twist_im = jnp.sin(angles)
    band_ids = jnp.arange(band_count, dtype=jnp.int32)
    band_turns = (phase_ids[:, None] * band_ids[None, :]) % PHASES
    band_angles = band_turns.astype(jnp.float32) * jnp.float32(-2.0 * math.pi / PHASES)
    band_re = jnp.cos(band_angles)
    band_im = jnp.sin(band_angles)
    block_len = math.gcd(inputs, 32)
    highest = lax.Precision.HIGHEST

    def channelise(shard_piece):
        widened = shard_piece.astype(jnp.float32)
        filtered = jnp.zeros((block_len, spectra_count, PHASES, SLOTS), jnp.float32)
        for tap_index in range(TAPS):
            first_row = TAPS - 1 - tap_index
            filtered = filtered + fir_taps[:, tap_index, :] * widened[:, first_row:first_row + spectra_count]
        spectrum = jnp.fft.fft(filtered, axis=-1)
        part_re = spectrum.real
        part_im = spectrum.imag
        branch_re = (part_re * twist_re - part_im * twist_im).astype(jnp.bfloat16)
        branch_im = (part_re * twist_im + part_im * twist_re).astype(jnp.bfloat16)
        branch_re = lax.optimization_barrier(branch_re).astype(jnp.float32)
        branch_im = lax.optimization_barrier(branch_im).astype(jnp.float32)
        einsum_form = 'nspk,pb->nsbk'
        spec_re = jnp.einsum(einsum_form, branch_re, band_re, precision=highest) - jnp.einsum(einsum_form, branch_im, band_im, precision=highest)
        spec_im = jnp.einsum(einsum_form, branch_re, band_im, precision=highest) + jnp.einsum(einsum_form, branch_im, band_re, precision=highest)
        return spec_re.astype(jnp.bfloat16), spec_im.astype(jnp.bfloat16)

    pieces = ordered.reshape(inputs // block_len, block_len, frames, PHASES, SLOTS)
    spec_re, spec_im = lax.map(channelise, pieces)
    spec_re = spec_re.reshape(inputs, spectra_count, band_count, SLOTS)
    spec_im = spec_im.reshape(inputs, spectra_count, band_count, SLOTS)
    subs = SLOTS // AVG
    scaling = 1.0 / (frame_len * AVG * spectra_count)

    def correlate(flat_index):
        band_at = flat_index // subs
        sub_at = flat_index % subs
        zero_at = jnp.int32(0)
        corner = (zero_at, zero_at, band_at.astype(jnp.int32), (sub_at * AVG).astype(jnp.int32))
        sizes = (inputs, spectra_count, 1, AVG)
        left_re = lax.dynamic_slice(spec_re, corner, sizes).reshape(inputs, spectra_count * AVG)
        left_im = lax.dynamic_slice(spec_im, corner, sizes).reshape(inputs, spectra_count * AVG)
        vis_re = jnp.dot(left_re, left_re.T, preferred_element_type=jnp.float32) + jnp.dot(left_im, left_im.T, preferred_element_type=jnp.float32)
        vis_im = jnp.dot(left_im, left_re.T, preferred_element_type=jnp.float32) - jnp.dot(left_re, left_im.T, preferred_element_type=jnp.float32)
        return jnp.stack([vis_re, vis_im]) * scaling

    result = lax.map(correlate, jnp.arange(band_count * subs, dtype=jnp.int32))
    return result.reshape(band_count, subs, 2, inputs, inputs)
```

```python
import functools
import math

import jax
import jax.numpy as jnp
from jax import lax
from jax.experimental import pallas as pl
from jax.experimental.pallas import tpu as pltpu
from jax.sharding import PartitionSpec as P

AVG = 16
LANES = 128


def shifted(block, axis, distance):
    devices = range(lax.axis_size(axis))
    route = [(i - distance, i) for i in devices if i - distance in devices]
    return lax.ppermute(block, axis, route)


def rotation(numbers, modulus):
    angles = (numbers % modulus).astype(jnp.float32) * jnp.float32(-2.0 * math.pi / modulus)
    return (jnp.cos(angles), jnp.sin(angles))


def split_pair(table):
    upper = table.astype(jnp.bfloat16)
    lower = (table - upper.astype(jnp.float32)).astype(jnp.bfloat16)
    return (upper, lower)


def complex_table(real_part, imag_part, axis_at):
    first = jnp.stack([real_part, imag_part], axis=-1)
    second = jnp.stack([-imag_part, real_part], axis=-1)
    return jnp.stack([first, second], axis=axis_at)


def all_frames(voltages, fir_taps):
    inputs_dev, _, frames_dev, slot_count = voltages.shape
    phases = fir_taps.shape[0]
    tap_count = fir_taps.shape[1]
    lane_count = lax.axis_size("chan")
    groups = lane_count // phases
    position = lax.axis_index("chan")
    my_phase = position % phases
    my_group = position // phases
    recent = voltages[:, 0]
    if groups > 1:
        earlier = shifted(voltages[:, 0, frames_dev - (tap_count - 1) :, :], "chan", phases)
    else:
        earlier = jnp.zeros((inputs_dev, tap_count - 1, slot_count), voltages.dtype)
    series = jnp.concatenate([earlier, recent], axis=1)
    coeffs = lax.dynamic_index_in_dim(fir_taps, my_phase, 0, keepdims=False)
    frame_ids = my_group * frames_dev + jnp.arange(frames_dev, dtype=jnp.int32)
    keep_mask = (frame_ids >= tap_count - 1).astype(jnp.float32)
    filtered = sum(
        (
            coeffs[tap_index]
            * series[:, tap_count - 1 - tap_index : tap_count - 1 - tap_index + frames_dev].astype(
                jnp.float32
            )
            for tap_index in range(tap_count)
        )
    )
    filtered = filtered * keep_mask[None, :, None]
    better = lax.Precision.HIGH
    split_len = slot_count // phases
    folded = filtered.reshape(inputs_dev, frames_dev, split_len, phases)
    slot_ids = jnp.arange(split_len, dtype=jnp.int32)
    short_re, short_im = rotation(slot_ids[:, None] * slot_ids[None, :], split_len)
    short_table = jnp.stack([short_re, short_im], axis=-1)
    inner = jnp.einsum(
        "ifqr,qvc->rvcfi", folded, short_table, precision=better, preferred_element_type=jnp.float32
    )
    rest_ids = jnp.arange(phases, dtype=jnp.int32)
    freq_ids = jnp.arange(slot_count, dtype=jnp.int32).reshape(phases, split_len)
    twist_re, twist_im = rotation(
        (my_phase + phases * rest_ids)[:, None, None] * freq_ids[None], phases * slot_count
    )
    twist_table = complex_table(twist_re, twist_im, 3)
    branch = jnp.einsum(
        "rvcfi,ruvcd->uvfdi",
        inner,
        twist_table,
        precision=better,
        preferred_element_type=jnp.float32,
    )
    branch = branch.reshape(slot_count, 1, frames_dev, 2, inputs_dev).astype(jnp.bfloat16)
    band_count = phases // 2
    band_re, band_im = rotation(
        rest_ids[:, None] * jnp.arange(band_count, dtype=jnp.int32)[None, :], phases
    )
    band_table = complex_table(band_re, band_im, 1)
    band_upper, band_lower = split_pair(band_table)
    turned = lax.all_to_all(branch, "chan", split_axis=0, concat_axis=1, tiled=True)
    span_len = turned.shape[0]
    sources = turned.shape[1]
    item_count = turned.shape[2]
    grouped = turned.reshape(span_len, sources // phases, phases, item_count, 2, inputs_dev)
    phase_form = "wgpfci,pcbd->bwgfdi"
    total = jnp.einsum(
        phase_form, grouped, band_upper, preferred_element_type=jnp.float32
    ) + jnp.einsum(phase_form, grouped, band_lower, preferred_element_type=jnp.float32)
    spectra = total.astype(jnp.bfloat16)
    span_dev = spectra.shape[1]
    subs_dev = span_dev // AVG
    stacked = spectra.reshape(band_count, subs_dev, AVG * groups * frames_dev, 2, inputs_dev)
    columns = stacked.reshape(band_count, subs_dev, -1, inputs_dev)
    swapped = jnp.stack([stacked[:, :, :, 1], -stacked[:, :, :, 0]], axis=3).reshape(
        band_count, subs_dev, -1, inputs_dev
    )
    left_side = jnp.stack([columns, swapped], axis=2)
    spectra_count = groups * frames_dev - (tap_count - 1)
    scaling = 1.0 / (phases * slot_count * AVG * spectra_count)
    vis_form = "bsokn,bskw->bsonw"
    return (
        jnp.einsum(
            vis_form,
            left_side,
            lax.all_gather(columns, "stn", axis=3, tiled=True),
            preferred_element_type=jnp.float32,
        )
        * scaling
    )


def split_value(value):
    upper = value.astype(jnp.bfloat16)
    lower = (value - upper.astype(jnp.float32)).astype(jnp.bfloat16)
    return upper, lower


def weighted(terms, weights):
    total = None
    for term, weight in zip(terms, weights):
        if abs(weight) < 1e-9:
            continue
        if abs(abs(weight) - 1.0) < 1e-9:
            part, negative = term, weight < 0
        else:
            part, negative = term * jnp.float32(abs(weight)), weight < 0
        if total is None:
            total = -part if negative else part
        else:
            total = total - part if negative else total + part
    return total


def turn_weights(count, step, radix):
    angles = [-2.0 * math.pi * ((k * step) % radix) / radix for k in range(count)]
    return [math.cos(a) for a in angles], [math.sin(a) for a in angles]


def half_sums(pieces):
    half = len(pieces) // 2
    sums = [pieces[k] + pieces[k + half] for k in range(half)]
    differences = [pieces[k] - pieces[k + half] for k in range(half)]
    return sums, differences


def branch_kernel(radix, phase_ref, volt_ref, taps_ref, cos_ref, sin_ref, low_ref, out_ref, y_hi, y_lo):
    step = pl.program_id(0)
    rows = volt_ref.shape[0]
    tap_count = taps_ref.shape[1]
    taps = taps_ref[0]
    by_frame = jnp.concatenate([taps[k : k + 1] for k in reversed(range(tap_count))], axis=0)
    filtered = jnp.sum(volt_ref[:, 0].astype(jnp.float32) * by_frame[None], axis=1)
    pieces = [filtered[:, a * LANES : (a + 1) * LANES] for a in range(radix)]
    sums, differences = half_sums(pieces)
    at = pl.ds(pl.multiple_of(step * rows, rows), rows)
    for u in range(radix // 2 + 1):
        terms = differences if u % 2 else sums
        re_weights, im_weights = turn_weights(radix // 2, u, radix)
        for part, weights in enumerate((re_weights, im_weights)):
            value = weighted(terms, weights)
            if value is None:
                value = jnp.zeros_like(pieces[0])
            upper, lower = split_value(value)
            y_hi[u, at, part * LANES : (part + 1) * LANES] = upper
            y_lo[u, at, part * LANES : (part + 1) * LANES] = lower

    @pl.when(step == pl.num_programs(0) - 1)
    def _():
        form = (((1,), (1,)), ((), ()))
        for u in range(radix):
            source = min(u, radix - u)
            table = cos_ref[...] * low_ref[0, u : u + 1] - sin_ref[...] * low_ref[1, u : u + 1]
            upper, lower = split_value(table)
            total = lax.dot_general(upper, y_hi[source], form, preferred_element_type=jnp.float32)
            total += lax.dot_general(upper, y_lo[source], form, preferred_element_type=jnp.float32)
            total += lax.dot_general(lower, y_hi[source], form, preferred_element_type=jnp.float32)
            out_ref[:, u] = total.astype(jnp.bfloat16).reshape(out_ref.shape[0], *out_ref.shape[2:])


def branch_tables(phase, phases, radix, dests):
    slots = radix * LANES
    near = LANES // dests
    v_ids = jnp.arange(dests, dtype=jnp.int32)[:, None, None] * near + jnp.arange(near, dtype=jnp.int32)
    v_ids = jnp.broadcast_to(v_ids, (dests, 2, near)).reshape(-1, 1)
    quarter = phases * slots // 4
    row_part = jnp.broadcast_to(jnp.arange(2, dtype=jnp.int32)[None, :, None], (dests, 2, near)).reshape(-1, 1)
    column = jnp.arange(2 * LANES, dtype=jnp.int32)[None, :]
    lag = phase + phases * (column % LANES)
    turns = radix * v_ids * lag - quarter * (column // LANES) + quarter * row_part
    far_cos, far_sin = rotation(turns, phases * slots)
    u_ids = jnp.arange(radix, dtype=jnp.int32)[:, None]
    low_cos, low_sin = rotation(u_ids * lag, phases * slots)
    mirrored = (u_ids > radix // 2) & (column >= LANES)
    low = jnp.stack([low_cos, low_sin])
    return far_cos, far_sin, jnp.where(mirrored[None], -low, low)


def branch_of(voltages, fir_taps, dests):
    inputs, _, frames, slots = voltages.shape
    phases, tap_count, _ = fir_taps.shape
    radix = slots // LANES
    near = LANES // dests
    phase = lax.axis_index("chan") % phases
    far_cos, far_sin, low = branch_tables(phase, phases, radix, dests)
    block = math.gcd(inputs, 32)
    whole = lambda *shape: pl.BlockSpec(shape, lambda i, ph: (0,) * len(shape))
    return pl.pallas_call(
        functools.partial(branch_kernel, radix),
        out_shape=jax.ShapeDtypeStruct((dests, radix, 2 * near, inputs), jnp.bfloat16),
        grid_spec=pltpu.PrefetchScalarGridSpec(
            num_scalar_prefetch=1,
            grid=(inputs // block,),
            in_specs=[
                pl.BlockSpec((block, 1, frames, slots), lambda i, ph: (i, 0, 0, 0)),
                pl.BlockSpec((1, tap_count, slots), lambda i, ph: (ph[0], 0, 0)),
                whole(*far_cos.shape),
                whole(*far_sin.shape),
                whole(*low.shape),
            ],
            out_specs=whole(dests, radix, 2 * near, inputs),
            scratch_shapes=[pltpu.VMEM((radix // 2 + 1, inputs, 2 * LANES), jnp.bfloat16)] * 2,
        ),
        name="branch",
    )(phase.reshape(1), voltages, fir_taps, far_cos, far_sin, low)


def band_kernel(turned_ref, right_ref, left_ref, swapped):
    phases, radix, rows, inputs = turned_ref.shape
    near = rows // 2
    for u in range(radix):
        re = [turned_ref[p, u, :near].astype(jnp.float32) for p in range(phases)]
        im = [turned_ref[p, u, near:].astype(jnp.float32) for p in range(phases)]
        re_pair, im_pair = half_sums(re), half_sums(im)
        for c in range(phases // 2):
            cos_w, sin_w = turn_weights(phases // 2, c, phases)
            re_t, im_t = re_pair[c % 2], im_pair[c % 2]
            minus = [-w for w in sin_w]
            spec_re = weighted(re_t + im_t, cos_w + minus).astype(jnp.bfloat16)
            spec_im = weighted(re_t + im_t, sin_w + cos_w).astype(jnp.bfloat16)
            at = u * rows
            right_ref[c, at : at + near] = spec_re
            right_ref[c, at + near : at + rows] = spec_im
            swapped[c, at : at + near] = spec_im
            swapped[c, at + near : at + rows] = -spec_re
    for c in range(phases // 2):
        left_ref[0, c] = right_ref[c].T
        left_ref[1, c] = swapped[c].T


def bands_of(turned):
    phases, radix, rows, inputs = turned.shape
    bands, depth = phases // 2, radix * rows
    return pl.pallas_call(
        band_kernel,
        out_shape=(
            jax.ShapeDtypeStruct((bands, depth, inputs), jnp.bfloat16),
            jax.ShapeDtypeStruct((2, bands, inputs, depth), jnp.bfloat16),
        ),
        in_specs=[pl.BlockSpec(memory_space=pltpu.VMEM)],
        out_specs=[pl.BlockSpec(memory_space=pltpu.VMEM)] * 2,
        scratch_shapes=[pltpu.VMEM((bands, depth, inputs), jnp.bfloat16)],
        name="bands",
    )(turned)


def correlate_kernel(near, group, scaling, column_ref, left_ref, right_ref, *rest):
    out_ref = rest[-1]
    subs = out_ref.shape[1]
    first = pl.program_id(1) * subs
    depth = left_ref.shape[-1]
    lanes = lax.broadcasted_iota(jnp.int32, (16, depth), 1) % near // group
    for k in range(subs):
        mask = (lanes == first + k).astype(jnp.float32).astype(jnp.bfloat16)[:1]
        for part in range(2):
            product = jnp.dot(left_ref[part, 0] * mask, right_ref[0], preferred_element_type=jnp.float32)
            out_ref[0, k, part] = product * scaling


def correlate(left, right, column, total, near, radix, scaling, shape):
    _, bands, inputs, depth = left.shape
    group = AVG // radix
    subs = near // group
    block = math.gcd(subs, 2)
    fresh = total is None
    return pl.pallas_call(
        functools.partial(correlate_kernel, near, group, scaling),
        out_shape=jax.ShapeDtypeStruct(shape, jnp.float32),
        grid_spec=pltpu.PrefetchScalarGridSpec(
            num_scalar_prefetch=1,
            grid=(bands, subs // block),
            in_specs=[
                pl.BlockSpec((2, 1, inputs, depth), lambda c, j, col: (0, c, 0, 0)),
                pl.BlockSpec((1, depth, inputs), lambda c, j, col: (c, 0, 0)),
            ]
            + ([] if fresh else [pl.BlockSpec(memory_space=pl.ANY)]),
            out_specs=pl.BlockSpec((1, block, 2, inputs, inputs), lambda c, j, col: (c, j, 0, 0, col[0])),
        ),
        input_output_aliases={} if fresh else {3: 0},
        name="correlate",
    )(*((column.reshape(1), left, right) + (() if fresh else (total,))))


def one_frame(voltages, fir_taps):
    inputs, _, frames, slots = voltages.shape
    phases = fir_taps.shape[0]
    dests = lax.axis_size("chan")
    radix = slots // LANES
    near = LANES // dests
    branch = branch_of(voltages, fir_taps, dests)
    turned = lax.all_to_all(branch, "chan", split_axis=0, concat_axis=0, tiled=True)
    right, left = bands_of(turned)
    stations = lax.axis_size("stn")
    me = lax.axis_index("stn")
    ring = [(i, (i + 1) % stations) for i in range(stations)]
    bands = phases // 2
    shape = (bands, near * radix // AVG, 2, inputs, inputs * stations)
    scaling = 1.0 / (phases * slots * AVG)
    total = None
    for hop in range(stations):
        later = lax.ppermute(right, "stn", ring) if hop < stations - 1 else None
        column = (me - hop) % stations
        total = correlate(left, right, column, total, near, radix, scaling, shape)
        right = later
    return total


def per_device(voltages, fir_taps):
    inputs, _, frames, slots = voltages.shape
    phases, tap_count, _ = fir_taps.shape
    lanes = lax.axis_size("chan")
    radix = slots // LANES
    fits = (
        lanes == phases
        and frames == tap_count
        and phases % 2 == 0
        and slots % LANES == 0
        and radix % 2 == 0
        and AVG % radix == 0
        and LANES % (16 * lanes) == 0
        and inputs % LANES == 0
    )
    return one_frame(voltages, fir_taps) if fits else all_frames(voltages, fir_taps)


def solution(mesh):
    return jax.shard_map(
        per_device,
        mesh=mesh,
        in_specs=(P("stn", "chan", None, None), P()),
        out_specs=P(None, "chan", None, "stn", None),
        check_vma=False,
    )
```

```python
import functools
import math

import jax
import jax.numpy as jnp
import numpy as np
from jax import lax
from jax.experimental import pallas as pl
from jax.experimental.pallas import tpu as pltpu
from jax.sharding import PartitionSpec as P

AVG = 16
LANES = 128
PER_PART = 2
SLOTS_OUT = 8


def shifted(block, axis, distance):
    devices = range(lax.axis_size(axis))
    route = [(i - distance, i) for i in devices if i - distance in devices]
    return lax.ppermute(block, axis, route)


def rotation(numbers, modulus):
    angles = (numbers % modulus).astype(jnp.float32) * jnp.float32(-2.0 * math.pi / modulus)
    return (jnp.cos(angles), jnp.sin(angles))


def split_pair(table):
    upper = table.astype(jnp.bfloat16)
    lower = (table - upper.astype(jnp.float32)).astype(jnp.bfloat16)
    return (upper, lower)


def complex_table(real_part, imag_part, axis_at):
    first = jnp.stack([real_part, imag_part], axis=-1)
    second = jnp.stack([-imag_part, real_part], axis=-1)
    return jnp.stack([first, second], axis=axis_at)


def all_frames(voltages, fir_taps):
    inputs_dev, _, frames_dev, slot_count = voltages.shape
    phases = fir_taps.shape[0]
    tap_count = fir_taps.shape[1]
    lane_count = lax.axis_size("chan")
    groups = lane_count // phases
    position = lax.axis_index("chan")
    my_phase = position % phases
    my_group = position // phases
    recent = voltages[:, 0]
    if groups > 1:
        earlier = shifted(voltages[:, 0, frames_dev - (tap_count - 1) :, :], "chan", phases)
    else:
        earlier = jnp.zeros((inputs_dev, tap_count - 1, slot_count), voltages.dtype)
    series = jnp.concatenate([earlier, recent], axis=1)
    coeffs = lax.dynamic_index_in_dim(fir_taps, my_phase, 0, keepdims=False)
    frame_ids = my_group * frames_dev + jnp.arange(frames_dev, dtype=jnp.int32)
    keep_mask = (frame_ids >= tap_count - 1).astype(jnp.float32)
    filtered = sum(
        (
            coeffs[tap_index]
            * series[:, tap_count - 1 - tap_index : tap_count - 1 - tap_index + frames_dev].astype(
                jnp.float32
            )
            for tap_index in range(tap_count)
        )
    )
    filtered = filtered * keep_mask[None, :, None]
    better = lax.Precision.HIGH
    split_len = slot_count // phases
    folded = filtered.reshape(inputs_dev, frames_dev, split_len, phases)
    slot_ids = jnp.arange(split_len, dtype=jnp.int32)
    short_re, short_im = rotation(slot_ids[:, None] * slot_ids[None, :], split_len)
    short_table = jnp.stack([short_re, short_im], axis=-1)
    inner = jnp.einsum(
        "ifqr,qvc->rvcfi", folded, short_table, precision=better, preferred_element_type=jnp.float32
    )
    rest_ids = jnp.arange(phases, dtype=jnp.int32)
    freq_ids = jnp.arange(slot_count, dtype=jnp.int32).reshape(phases, split_len)
    twist_re, twist_im = rotation(
        (my_phase + phases * rest_ids)[:, None, None] * freq_ids[None], phases * slot_count
    )
    twist_table = complex_table(twist_re, twist_im, 3)
    branch = jnp.einsum(
        "rvcfi,ruvcd->uvfdi",
        inner,
        twist_table,
        precision=better,
        preferred_element_type=jnp.float32,
    )
    branch = branch.reshape(slot_count, 1, frames_dev, 2, inputs_dev).astype(jnp.bfloat16)
    band_count = phases // 2
    band_re, band_im = rotation(
        rest_ids[:, None] * jnp.arange(band_count, dtype=jnp.int32)[None, :], phases
    )
    band_table = complex_table(band_re, band_im, 1)
    band_upper, band_lower = split_pair(band_table)
    turned = lax.all_to_all(branch, "chan", split_axis=0, concat_axis=1, tiled=True)
    span_len = turned.shape[0]
    sources = turned.shape[1]
    item_count = turned.shape[2]
    grouped = turned.reshape(span_len, sources // phases, phases, item_count, 2, inputs_dev)
    phase_form = "wgpfci,pcbd->bwgfdi"
    total = jnp.einsum(
        phase_form, grouped, band_upper, preferred_element_type=jnp.float32
    ) + jnp.einsum(phase_form, grouped, band_lower, preferred_element_type=jnp.float32)
    spectra = total.astype(jnp.bfloat16)
    span_dev = spectra.shape[1]
    subs_dev = span_dev // AVG
    stacked = spectra.reshape(band_count, subs_dev, AVG * groups * frames_dev, 2, inputs_dev)
    columns = stacked.reshape(band_count, subs_dev, -1, inputs_dev)
    swapped = jnp.stack([stacked[:, :, :, 1], -stacked[:, :, :, 0]], axis=3).reshape(
        band_count, subs_dev, -1, inputs_dev
    )
    left_side = jnp.stack([columns, swapped], axis=2)
    spectra_count = groups * frames_dev - (tap_count - 1)
    scaling = 1.0 / (phases * slot_count * AVG * spectra_count)
    vis_form = "bsokn,bskw->bsonw"
    return (
        jnp.einsum(
            vis_form,
            left_side,
            lax.all_gather(columns, "stn", axis=3, tiled=True),
            preferred_element_type=jnp.float32,
        )
        * scaling
    )


def split_value(value):
    upper = value.astype(jnp.bfloat16)
    lower = (value - upper.astype(jnp.float32)).astype(jnp.bfloat16)
    return upper, lower


def weighted(terms, weights):
    total = None
    for term, weight in zip(terms, weights):
        if abs(weight) < 1e-9:
            continue
        part = term if abs(abs(weight) - 1.0) < 1e-9 else term * jnp.float32(abs(weight))
        if total is None:
            total = -part if weight < 0 else part
        else:
            total = total - part if weight < 0 else total + part
    return total


def turn_weights(count, step, radix):
    angles = [-2.0 * math.pi * ((k * step) % radix) / radix for k in range(count)]
    return [math.cos(a) for a in angles], [math.sin(a) for a in angles]


def half_sums(pieces):
    half = len(pieces) // 2
    sums = [pieces[k] + pieces[k + half] for k in range(half)]
    differences = [pieces[k] - pieces[k + half] for k in range(half)]
    return sums, differences


def branch_tables(phases, radix, dests):
    slots = radix * LANES
    near = LANES // dests
    v = np.repeat(np.arange(LANES).reshape(dests, 1, near), 2, axis=1).reshape(-1, 1)
    is_imag = np.broadcast_to(np.arange(2)[None, :, None], (dests, 2, near)).reshape(-1, 1)
    column = np.arange(2 * LANES)[None, :]
    b, half = column % LANES, column // LANES
    angle = -2.0 * np.pi * ((v * b) % LANES) / LANES + 0.5 * np.pi * (half - is_imag)
    far = np.stack([np.cos(angle), np.sin(angle)])
    phase = np.arange(phases)
    angle = -2.0 * np.pi * ((v * phase[None, :]) % slots) / slots
    row = np.stack([np.cos(angle), np.sin(angle)], axis=1).transpose(2, 0, 1)
    row = np.broadcast_to(row[..., None], row.shape + (1,))
    u = np.arange(radix)[None, :, None]
    turns = (u * (phase[:, None, None] + phases * b[None])) % (phases * slots)
    angle = -2.0 * np.pi * turns / (phases * slots)
    low = np.stack([np.cos(angle), np.sin(angle)], axis=1)
    mirrored = (u > radix // 2) & (half[None] == 1)
    low = np.where(mirrored[:, None], -low, low)
    return far.astype(np.float32), row[..., 0].astype(np.float32), low.astype(np.float32)


def branch_kernel(radix, dests, place_ref, volt_ref, taps_ref, far_ref, row_ref, low_ref, *rest):
    outs, (volts, y, table, block, volt_sems, out_sems) = rest[:-6], rest[-6:]
    me = place_ref[0]
    parts, rows = volts.shape[0], volts.shape[1]
    loads = [
        pltpu.make_async_copy(volt_ref.at[pl.ds(i * rows, rows), 0], volts.at[i], volt_sems.at[i])
        for i in range(parts)
    ]
    for load in loads:
        load.start()
    row_cos, row_sin = row_ref[0, :, 0:1], row_ref[0, :, 1:2]
    far_cos = far_ref[0] * row_cos - far_ref[1] * row_sin
    far_sin = far_ref[0] * row_sin + far_ref[1] * row_cos
    for u in range(radix):
        entry = far_cos * low_ref[0, 0, u : u + 1] - far_sin * low_ref[0, 1, u : u + 1]
        table[0, u], table[1, u] = split_value(entry)
    taps = taps_ref[0]
    by_frame = jnp.concatenate([taps[k : k + 1] for k in reversed(range(taps.shape[0]))], axis=0)
    together = LANES // rows
    for i in range(0, parts, together):
        filtered = []
        for k in range(i, i + together):
            loads[k].wait()
            filtered.append(jnp.sum(volts[k].astype(jnp.float32) * by_frame[None], axis=1))
        filtered = jnp.concatenate(filtered, axis=0)
        pieces = [filtered[:, a * LANES : (a + 1) * LANES].T for a in range(radix)]
        sums, differences = half_sums(pieces)
        for u in range(radix // 2 + 1):
            terms = differences if u % 2 else sums
            for part, weights in enumerate(turn_weights(radix // 2, u, radix)):
                value = weighted(terms, weights)
                if value is None:
                    value = jnp.zeros_like(pieces[0])
                at = (pl.ds(part * LANES, LANES), pl.ds(i * rows, LANES))
                y[(u, 0) + at], y[(u, 1) + at] = split_value(value)
    inputs = y.shape[3]
    for u in range(radix):
        source = min(u, radix - u)
        total = jnp.dot(table[0, u], y[source, 0], preferred_element_type=jnp.float32)
        total += jnp.dot(table[0, u], y[source, 1], preferred_element_type=jnp.float32)
        total += jnp.dot(table[1, u], y[source, 0], preferred_element_type=jnp.float32)
        block[:, u] = total.astype(jnp.bfloat16).reshape(dests, -1, inputs)
    stores = []
    for k in range(dests):
        dest = lax.bitwise_xor(me, k)
        stores.append(pltpu.make_async_copy(block.at[dest], outs[k], out_sems.at[k]))
        stores[-1].start()
    for store in stores:
        store.wait()


def branch_of(voltages, fir_taps, me, dests):
    inputs, _, frames, slots = voltages.shape
    phases, tap_count, _ = fir_taps.shape
    radix = slots // LANES
    rows = LANES // dests
    far, row, low = branch_tables(phases, radix, dests)
    parts = 8
    block = inputs // parts
    place = lambda *shape: pl.BlockSpec((1,) + shape, lambda i, ph: (ph[0],) + (0,) * len(shape))
    outs = dests
    return pl.pallas_call(
        functools.partial(branch_kernel, radix, dests),
        out_shape=[jax.ShapeDtypeStruct((radix, 2 * rows, inputs), jnp.bfloat16)] * outs,
        grid_spec=pltpu.PrefetchScalarGridSpec(
            num_scalar_prefetch=1,
            grid=(1,),
            in_specs=[
                pl.BlockSpec(memory_space=pl.ANY),
                place(tap_count, slots),
                pl.BlockSpec(far.shape, lambda i, ph: (0, 0, 0)),
                place(*row.shape[1:]),
                place(*low.shape[1:]),
            ],
            out_specs=[pl.BlockSpec(memory_space=pl.ANY)] * outs,
            scratch_shapes=[
                pltpu.VMEM((parts, block, frames, slots), jnp.bfloat16),
                pltpu.VMEM((radix // 2 + 1, 2, 2 * LANES, inputs), jnp.bfloat16),
                pltpu.VMEM((2, radix, 2 * LANES, 2 * LANES), jnp.bfloat16),
                pltpu.VMEM((dests, radix, 2 * rows, inputs), jnp.bfloat16),
                pltpu.SemaphoreType.DMA((parts,)),
                pltpu.SemaphoreType.DMA((outs,)),
            ],
        ),
        cost_estimate=pl.CostEstimate(
            flops=6 * radix * inputs * (2 * LANES) ** 2,
            transcendentals=0,
            bytes_accessed=2 * voltages.size + 4 * inputs * slots,
        ),
        name="branch",
    )(me.reshape(1), voltages, fir_taps, far, row, low)


def band_kernel(place_ref, *rest):
    turned, sems = rest[-2:]
    phases, radix, rows, _ = turned.shape
    blocks, outs = rest[:phases], rest[phases:-2]
    me = place_ref[0]
    loads = [
        pltpu.make_async_copy(blocks[k], turned.at[lax.bitwise_xor(me, k)], sems.at[k]) for k in range(phases)
    ]
    for load in loads:
        load.start()
    for load in loads:
        load.wait()
    near = rows // 2
    for u in range(radix):
        pair = [turned[p, u].astype(jnp.float32) for p in range(phases)]
        re, im = [x[:near] for x in pair], [x[near:] for x in pair]
        re_pair, im_pair = half_sums(re), half_sums(im)
        at = u * rows
        for c in range(phases // 2):
            cos_w, sin_w = turn_weights(phases // 2, c, phases)
            terms = re_pair[c % 2] + im_pair[c % 2]
            out_ref, band = outs[c // PER_PART], c % PER_PART
            out_ref[band, at : at + near] = weighted(terms, cos_w + [-w for w in sin_w]).astype(jnp.bfloat16)
            out_ref[band, at + near : at + rows] = weighted(terms, sin_w + cos_w).astype(jnp.bfloat16)


def bands_of(blocks, me):
    phases = len(blocks)
    radix, rows, inputs = blocks[0].shape
    bands, depth = phases // 2, radix * rows
    return pl.pallas_call(
        band_kernel,
        out_shape=[jax.ShapeDtypeStruct((PER_PART, depth, inputs), jnp.bfloat16)] * (bands // PER_PART),
        in_specs=[pl.BlockSpec(memory_space=pltpu.SMEM)] + [pl.BlockSpec(memory_space=pl.ANY)] * phases,
        out_specs=[pl.BlockSpec(memory_space=pltpu.VMEM)] * (bands // PER_PART),
        scratch_shapes=[
            pltpu.VMEM((phases, radix, rows, inputs), jnp.bfloat16),
            pltpu.SemaphoreType.DMA((phases,)),
        ],
        cost_estimate=pl.CostEstimate(flops=0, transcendentals=0, bytes_accessed=6 * bands * depth * inputs),
        name="bands",
    )(me.reshape(1), *blocks)


def left_kernel(near, *refs):
    rights, left_ref = refs[:-1], refs[-1]
    for c in range(left_ref.shape[1]):
        right = rights[c // PER_PART][c % PER_PART]
        turned = right.astype(jnp.float32).T
        left_ref[0, c] = turned.astype(jnp.bfloat16)
        depth = turned.shape[1]
        real = lax.broadcasted_iota(jnp.int32, turned.shape, 1) % (2 * near) < near
        ahead = pltpu.roll(turned, depth - near, 1)
        behind = pltpu.roll(turned, near, 1)
        left_ref[1, c] = jnp.where(real, ahead, -behind).astype(jnp.bfloat16)


def left_of(rights, near):
    _, depth, inputs = rights[0].shape
    bands = PER_PART * len(rights)
    return pl.pallas_call(
        functools.partial(left_kernel, near),
        out_shape=jax.ShapeDtypeStruct((2, bands, inputs, depth), jnp.bfloat16),
        in_specs=[pl.BlockSpec(memory_space=pltpu.VMEM)] * len(rights),
        out_specs=pl.BlockSpec(memory_space=pltpu.VMEM),
        cost_estimate=pl.CostEstimate(flops=0, transcendentals=0, bytes_accessed=6 * bands * depth * inputs),
        name="left",
    )(*rights)


def correlate_kernel(near, group, parts, either, scaling, place_ref, left_ref, *rest):
    out_ref, buffer, sems = rest[-3:]
    rights = rest[: len(parts) * either]
    slots, _, _, width = buffer.shape
    depth = left_ref.shape[3]
    subs = near // group
    lanes = lax.broadcasted_iota(jnp.int32, (16, depth), 1) % near // group
    columns = pl.ds(pl.multiple_of(place_ref[0] * width, width), width)

    def store(c, k, slot):
        return pltpu.make_async_copy(buffer.at[slot], out_ref.at[c, k, :, :, columns], sems.at[slot])

    pending = [None] * slots
    for at, part in enumerate(parts):
        for band in range(PER_PART):
            c = part * PER_PART + band
            right = rights[at * either][band]
            if either > 1:
                right = jnp.where(place_ref[1] > 0, right, rights[at * either + 1][band])
            for k in range(subs):
                slot = ((at * PER_PART + band) * subs + k) % slots
                if pending[slot] is not None:
                    pending[slot].wait()
                mask = (lanes == k).astype(jnp.float32).astype(jnp.bfloat16)[:1]
                for half in range(2):
                    product = jnp.dot(left_ref[half, c] * mask, right, preferred_element_type=jnp.float32)
                    buffer[slot, half] = product * scaling
                pending[slot] = store(c, k, slot)
                pending[slot].start()
    for copy in pending:
        copy.wait()


def correlate(left, parts, rights, place, total, near, radix, scaling, shape):
    _, _, inputs, depth = left.shape
    group = AVG // radix
    subs = near // group
    fresh = total is None
    either = len(rights[0])
    flat = [right for pair in rights for right in pair]
    done = len(parts) * PER_PART
    return pl.pallas_call(
        functools.partial(correlate_kernel, near, group, tuple(parts), either, scaling),
        out_shape=jax.ShapeDtypeStruct(shape, jnp.float32),
        in_specs=[pl.BlockSpec(memory_space=pltpu.SMEM)]
        + [pl.BlockSpec(memory_space=pltpu.VMEM)] * (1 + len(flat))
        + ([] if fresh else [pl.BlockSpec(memory_space=pl.ANY)]),
        out_specs=pl.BlockSpec(memory_space=pl.ANY),
        scratch_shapes=[
            pltpu.VMEM((SLOTS_OUT, 2, inputs, inputs), jnp.float32),
            pltpu.SemaphoreType.DMA((SLOTS_OUT,)),
        ],
        input_output_aliases={} if fresh else {2 + len(flat): 0},
        cost_estimate=pl.CostEstimate(
            flops=4 * done * subs * inputs * inputs * depth,
            transcendentals=0,
            bytes_accessed=8 * done * subs * inputs * inputs,
        ),
        name="correlate",
    )(*([place, left] + flat + ([] if fresh else [total])))


def near_memory(array):
    return pltpu.with_memory_space_constraint(array, pltpu.VMEM)


def far_memory(array):
    return pltpu.with_memory_space_constraint(array, pltpu.HBM)


def one_frame(voltages, fir_taps):
    inputs, _, _, slots = voltages.shape
    phases = fir_taps.shape[0]
    dests = lax.axis_size("chan")
    radix = slots // LANES
    near = LANES // dests
    place = lax.axis_index("chan")
    branch = branch_of(voltages, fir_taps, place, dests)
    turned = [branch[0]] + [None] * (dests - 1)
    for k in reversed(range(1, dests)):
        turned[k] = far_memory(lax.ppermute(branch[k], "chan", [(i, i ^ k) for i in range(dests)]))
    own = bands_of(turned, place)
    parts = list(range(len(own)))
    stations = lax.axis_size("stn")
    me = lax.axis_index("stn")
    shape = (phases // 2, near * radix // AVG, 2, inputs, inputs * stations)
    scaling = 1.0 / (phases * slots * AVG)
    inner = (me == 1) | (me == 2)
    add = functools.partial(correlate, near=near, radix=radix, scaling=scaling, shape=shape)

    def spot(k):
        return jnp.stack([me ^ k, inner.astype(jnp.int32)])

    two = [near_memory(lax.ppermute(x, "stn", [(i, i ^ 2) for i in range(4)])) for x in own]
    one = [near_memory(lax.ppermute(x, "stn", [(i, i ^ 1) for i in range(4)])) for x in own]
    middle = [near_memory(lax.ppermute(x, "stn", [(1, 2), (2, 1)])) for x in own]
    relay = [near_memory(lax.ppermute(x, "stn", [(1, 0), (2, 3)])) for x in two]
    left = left_of(own, near)
    total = add(left, parts, [[x] for x in own], spot(0), None)
    for h in parts:
        total = add(left, [h], [[two[h]]], spot(2), total)
    total = add(left, parts, [[x] for x in one], spot(1), total)
    for h in parts:
        total = add(left, [h], [[middle[h], relay[h]]], spot(3), total)
    return total


def per_device(voltages, fir_taps):
    inputs, _, frames, slots = voltages.shape
    phases, tap_count, _ = fir_taps.shape
    lanes = lax.axis_size("chan")
    radix = slots // LANES
    fits = (
        lanes == phases
        and frames == tap_count
        and phases & (phases - 1) == 0
        and phases % 2 == 0
        and slots % LANES == 0
        and radix % 2 == 0
        and AVG % radix == 0
        and LANES % (16 * lanes) == 0
        and phases // 2 % PER_PART == 0
        and lax.axis_size("stn") == 4
        and inputs % LANES == 0
    )
    return one_frame(voltages, fir_taps) if fits else all_frames(voltages, fir_taps)


def solution(mesh):
    return jax.shard_map(
        per_device,
        mesh=mesh,
        in_specs=(P("stn", "chan", None, None), P()),
        out_specs=P(None, "chan", None, "stn", None),
        check_vma=False,
    )
```

```python
import functools
import math

import jax
import jax.numpy as jnp
import numpy as np
from jax import lax
from jax.experimental import pallas as pl
from jax.experimental.pallas import tpu as pltpu
from jax.sharding import PartitionSpec as P

AVG = 16
LANES = 128
HALVES = 2
SLOTS_OUT = 4


def shifted(block, axis, distance):
    devices = range(lax.axis_size(axis))
    route = [(i - distance, i) for i in devices if i - distance in devices]
    return lax.ppermute(block, axis, route)


def rotation(numbers, modulus):
    angles = (numbers % modulus).astype(jnp.float32) * jnp.float32(-2.0 * math.pi / modulus)
    return (jnp.cos(angles), jnp.sin(angles))


def split_pair(table):
    upper = table.astype(jnp.bfloat16)
    lower = (table - upper.astype(jnp.float32)).astype(jnp.bfloat16)
    return (upper, lower)


def complex_table(real_part, imag_part, axis_at):
    first = jnp.stack([real_part, imag_part], axis=-1)
    second = jnp.stack([-imag_part, real_part], axis=-1)
    return jnp.stack([first, second], axis=axis_at)


def all_frames(voltages, fir_taps):
    inputs_dev, _, frames_dev, slot_count = voltages.shape
    phases = fir_taps.shape[0]
    tap_count = fir_taps.shape[1]
    lane_count = lax.axis_size("chan")
    groups = lane_count // phases
    position = lax.axis_index("chan")
    my_phase = position % phases
    my_group = position // phases
    recent = voltages[:, 0]
    if groups > 1:
        earlier = shifted(voltages[:, 0, frames_dev - (tap_count - 1) :, :], "chan", phases)
    else:
        earlier = jnp.zeros((inputs_dev, tap_count - 1, slot_count), voltages.dtype)
    series = jnp.concatenate([earlier, recent], axis=1)
    coeffs = lax.dynamic_index_in_dim(fir_taps, my_phase, 0, keepdims=False)
    frame_ids = my_group * frames_dev + jnp.arange(frames_dev, dtype=jnp.int32)
    keep_mask = (frame_ids >= tap_count - 1).astype(jnp.float32)
    filtered = sum(
        (
            coeffs[tap_index]
            * series[:, tap_count - 1 - tap_index : tap_count - 1 - tap_index + frames_dev].astype(
                jnp.float32
            )
            for tap_index in range(tap_count)
        )
    )
    filtered = filtered * keep_mask[None, :, None]
    better = lax.Precision.HIGH
    split_len = slot_count // phases
    folded = filtered.reshape(inputs_dev, frames_dev, split_len, phases)
    slot_ids = jnp.arange(split_len, dtype=jnp.int32)
    short_re, short_im = rotation(slot_ids[:, None] * slot_ids[None, :], split_len)
    short_table = jnp.stack([short_re, short_im], axis=-1)
    inner = jnp.einsum(
        "ifqr,qvc->rvcfi", folded, short_table, precision=better, preferred_element_type=jnp.float32
    )
    rest_ids = jnp.arange(phases, dtype=jnp.int32)
    freq_ids = jnp.arange(slot_count, dtype=jnp.int32).reshape(phases, split_len)
    twist_re, twist_im = rotation(
        (my_phase + phases * rest_ids)[:, None, None] * freq_ids[None], phases * slot_count
    )
    twist_table = complex_table(twist_re, twist_im, 3)
    branch = jnp.einsum(
        "rvcfi,ruvcd->uvfdi",
        inner,
        twist_table,
        precision=better,
        preferred_element_type=jnp.float32,
    )
    branch = branch.reshape(slot_count, 1, frames_dev, 2, inputs_dev).astype(jnp.bfloat16)
    band_count = phases // 2
    band_re, band_im = rotation(
        rest_ids[:, None] * jnp.arange(band_count, dtype=jnp.int32)[None, :], phases
    )
    band_table = complex_table(band_re, band_im, 1)
    band_upper, band_lower = split_pair(band_table)
    turned = lax.all_to_all(branch, "chan", split_axis=0, concat_axis=1, tiled=True)
    span_len = turned.shape[0]
    sources = turned.shape[1]
    item_count = turned.shape[2]
    grouped = turned.reshape(span_len, sources // phases, phases, item_count, 2, inputs_dev)
    phase_form = "wgpfci,pcbd->bwgfdi"
    total = jnp.einsum(
        phase_form, grouped, band_upper, preferred_element_type=jnp.float32
    ) + jnp.einsum(phase_form, grouped, band_lower, preferred_element_type=jnp.float32)
    spectra = total.astype(jnp.bfloat16)
    span_dev = spectra.shape[1]
    subs_dev = span_dev // AVG
    stacked = spectra.reshape(band_count, subs_dev, AVG * groups * frames_dev, 2, inputs_dev)
    columns = stacked.reshape(band_count, subs_dev, -1, inputs_dev)
    swapped = jnp.stack([stacked[:, :, :, 1], -stacked[:, :, :, 0]], axis=3).reshape(
        band_count, subs_dev, -1, inputs_dev
    )
    left_side = jnp.stack([columns, swapped], axis=2)
    spectra_count = groups * frames_dev - (tap_count - 1)
    scaling = 1.0 / (phases * slot_count * AVG * spectra_count)
    vis_form = "bsokn,bskw->bsonw"
    return (
        jnp.einsum(
            vis_form,
            left_side,
            lax.all_gather(columns, "stn", axis=3, tiled=True),
            preferred_element_type=jnp.float32,
        )
        * scaling
    )


def split_value(value):
    upper = value.astype(jnp.bfloat16)
    lower = (value - upper.astype(jnp.float32)).astype(jnp.bfloat16)
    return upper, lower


def weighted(terms, weights):
    total = None
    for term, weight in zip(terms, weights):
        if abs(weight) < 1e-9:
            continue
        part = term if abs(abs(weight) - 1.0) < 1e-9 else term * jnp.float32(abs(weight))
        if total is None:
            total = -part if weight < 0 else part
        else:
            total = total - part if weight < 0 else total + part
    return total


def turn_weights(count, step, radix):
    angles = [-2.0 * math.pi * ((k * step) % radix) / radix for k in range(count)]
    return [math.cos(a) for a in angles], [math.sin(a) for a in angles]


def half_sums(pieces):
    half = len(pieces) // 2
    sums = [pieces[k] + pieces[k + half] for k in range(half)]
    differences = [pieces[k] - pieces[k + half] for k in range(half)]
    return sums, differences


def branch_tables(phases, radix, dests):
    slots = radix * LANES
    near = LANES // dests
    rows = near // HALVES
    entry = np.arange(LANES).reshape(dests, HALVES, rows).transpose(1, 0, 2)
    v = np.repeat(entry[:, :, None], 2, axis=2).reshape(-1, 1)
    is_imag = np.broadcast_to(np.arange(2)[:, None], (HALVES, dests, 2, rows)).reshape(-1, 1)
    column = np.arange(2 * LANES)[None, :]
    b, half = column % LANES, column // LANES
    angle = -2.0 * np.pi * ((v * b) % LANES) / LANES + 0.5 * np.pi * (half - is_imag)
    far = np.stack([np.cos(angle), np.sin(angle)])
    phase = np.arange(phases)
    angle = -2.0 * np.pi * ((v * phase[None, :]) % slots) / slots
    row = np.stack([np.cos(angle), np.sin(angle)], axis=1).transpose(2, 0, 1)
    row = np.broadcast_to(row[..., None], row.shape + (1,))
    u = np.arange(radix)[None, :, None]
    turns = (u * (phase[:, None, None] + phases * b[None])) % (phases * slots)
    angle = -2.0 * np.pi * turns / (phases * slots)
    low = np.stack([np.cos(angle), np.sin(angle)], axis=1)
    mirrored = (u > radix // 2) & (half[None] == 1)
    low = np.where(mirrored[:, None], -low, low)
    return far.astype(np.float32), row[..., 0].astype(np.float32), low.astype(np.float32)


def table_copies(half, me, far_ref, row_ref, low_ref, far, row, low, sems):
    rows = pl.ds(half * far.shape[1], far.shape[1])
    pairs = ((far_ref.at[:, rows], far), (row_ref.at[me, rows], row), (low_ref.at[me], low))
    return [pltpu.make_async_copy(source, target, sems.at[i]) for i, (source, target) in enumerate(pairs)]


def make_table(me, dests, far, row, low, table):
    share = far.shape[1] // dests
    for k in range(dests):
        at = pl.ds(pl.multiple_of(lax.bitwise_xor(me, k) * share, share), share)
        row_cos, row_sin = row[at, 0:1], row[at, 1:2]
        far_cos = far[0, at] * row_cos - far[1, at] * row_sin
        far_sin = far[0, at] * row_sin + far[1, at] * row_cos
        for u in range(table.shape[1]):
            entry = far_cos * low[0, u : u + 1] - far_sin * low[1, u : u + 1]
            to = pl.ds(k * share, share)
            table[0, u, to], table[1, u, to] = split_value(entry)


def transform(table, y, outs):
    radix = table.shape[1]
    share = table.shape[2] // len(outs)
    for u in range(radix):
        source = min(u, radix - u)
        total = jnp.dot(table[0, u], y[source, 0], preferred_element_type=jnp.float32)
        total += jnp.dot(table[0, u], y[source, 1], preferred_element_type=jnp.float32)
        total += jnp.dot(table[1, u], y[source, 0], preferred_element_type=jnp.float32)
        total = total.astype(jnp.bfloat16)
        for k, out_ref in enumerate(outs):
            out_ref[u] = total[k * share : (k + 1) * share]


def first_kernel(radix, dests, place_ref, volt_ref, taps_ref, far_ref, row_ref, low_ref, *rest):
    outs = rest[:dests]
    y, volts, filtered, table, taps, far, row, low, volt_sems, sems = rest[dests:]
    me = place_ref[0]
    parts, rows = volts.shape[0], volts.shape[1]
    small = table_copies(0, me, far_ref, row_ref, low_ref, far, row, low, sems)
    small.append(pltpu.make_async_copy(taps_ref.at[me], taps, sems.at[3]))
    loads = [
        pltpu.make_async_copy(volt_ref.at[pl.ds(i * rows, rows), 0], volts.at[i], volt_sems.at[i])
        for i in range(parts)
    ]
    for load in small + loads:
        load.start()
    for load in small:
        load.wait()
    make_table(me, dests, far, row, low, table)
    by_frame = jnp.concatenate([taps[k : k + 1] for k in reversed(range(taps.shape[0]))], axis=0)
    together = LANES // rows
    for i, load in enumerate(loads):
        load.wait()
        filtered[pl.ds(i * rows, rows)] = jnp.sum(volts[i].astype(jnp.float32) * by_frame[None], axis=1)
        if (i + 1) % together:
            continue
        inputs = pl.ds((i + 1) * rows - LANES, LANES)
        pieces = [filtered[inputs, a * LANES : (a + 1) * LANES].T for a in range(radix)]
        sums, differences = half_sums(pieces)
        for u in range(radix // 2 + 1):
            terms = differences if u % 2 else sums
            for part, weights in enumerate(turn_weights(radix // 2, u, radix)):
                value = weighted(terms, weights)
                if value is None:
                    value = jnp.zeros_like(pieces[0])
                at = (pl.ds(part * LANES, LANES), inputs)
                y[(u, 0) + at], y[(u, 1) + at] = split_value(value)
    transform(table, y, outs)


def next_kernel(half, dests, place_ref, y, far_ref, row_ref, low_ref, *rest):
    outs = rest[:dests]
    table, far, row, low, sems = rest[dests:]
    me = place_ref[0]
    small = table_copies(half, me, far_ref, row_ref, low_ref, far, row, low, sems)
    for load in small:
        load.start()
    for load in small:
        load.wait()
    make_table(me, dests, far, row, low, table)
    transform(table, y, outs)


def branch_of(voltages, fir_taps, me, dests):
    inputs, _, frames, slots = voltages.shape
    phases, tap_count, _ = fir_taps.shape
    radix = slots // LANES
    rows = LANES // dests // HALVES
    far, row, low = branch_tables(phases, radix, dests)
    parts = 8
    here = far.shape[1] // HALVES
    whole, near = pl.BlockSpec(memory_space=pl.ANY), pl.BlockSpec(memory_space=pltpu.VMEM)
    place = pl.BlockSpec(memory_space=pltpu.SMEM)
    blocks = [pltpu.VMEM((radix, 2 * rows, inputs), jnp.bfloat16)] * dests
    y = pltpu.VMEM((radix // 2 + 1, 2, 2 * LANES, inputs), jnp.bfloat16)
    table = pltpu.VMEM((2, radix, here, 2 * LANES), jnp.bfloat16)
    small = [
        pltpu.VMEM((2, here, 2 * LANES), jnp.float32),
        pltpu.VMEM((here, row.shape[2]), jnp.float32),
        pltpu.VMEM(low.shape[1:], jnp.float32),
    ]
    flops = 6 * radix * inputs * 2 * LANES * here
    *first, y = pl.pallas_call(
        functools.partial(first_kernel, radix, dests),
        out_shape=blocks + [y],
        in_specs=[place] + [whole] * 5,
        out_specs=[near] * (dests + 1),
        scratch_shapes=[
            pltpu.VMEM((parts, inputs // parts, frames, slots), jnp.bfloat16),
            pltpu.VMEM((inputs, slots), jnp.float32),
            table,
            pltpu.VMEM((tap_count, slots), jnp.float32),
        ]
        + small
        + [pltpu.SemaphoreType.DMA((parts,)), pltpu.SemaphoreType.DMA((4,))],
        cost_estimate=pl.CostEstimate(flops=flops, transcendentals=0, bytes_accessed=2 * voltages.size),
        name="branch",
    )(me.reshape(1), voltages, fir_taps, far, row, low)
    y = near_memory(y)
    result = [first]
    for half in range(1, HALVES):
        result.append(
            pl.pallas_call(
                functools.partial(next_kernel, half, dests),
                out_shape=blocks,
                in_specs=[place, near] + [whole] * 3,
                out_specs=[near] * dests,
                scratch_shapes=[table] + small + [pltpu.SemaphoreType.DMA((3,))],
                cost_estimate=pl.CostEstimate(flops=flops, transcendentals=0, bytes_accessed=4 * far.size),
                name="branch_next",
            )(me.reshape(1), y, far, row, low)
        )
    return [[near_memory(x) for x in part] for part in result]


def band_kernel(place_ref, *rest):
    out_ref, turned, sems = rest[-3:]
    phases, radix, rows, _ = turned.shape
    blocks = rest[:phases]
    me = place_ref[0]
    loads = [
        pltpu.make_async_copy(blocks[k], turned.at[lax.bitwise_xor(me, k)], sems.at[k]) for k in range(phases)
    ]
    for load in loads:
        load.start()
    for load in loads:
        load.wait()
    near = rows // 2
    for u in range(radix):
        pair = [turned[p, u].astype(jnp.float32) for p in range(phases)]
        re_pair, im_pair = half_sums([x[:near] for x in pair]), half_sums([x[near:] for x in pair])
        for c in range(phases // 2):
            cos_w, sin_w = turn_weights(phases // 2, c, phases)
            terms = re_pair[c % 2] + im_pair[c % 2]
            spectrum = [weighted(terms, cos_w + [-w for w in sin_w]), weighted(terms, sin_w + cos_w)]
            out_ref[c, u * rows : (u + 1) * rows] = jnp.concatenate(spectrum, axis=0).astype(jnp.bfloat16)


def bands_of(blocks, me):
    phases = len(blocks)
    radix, rows, inputs = blocks[0].shape
    bands, depth = phases // 2, radix * rows
    return pl.pallas_call(
        band_kernel,
        out_shape=pltpu.VMEM((bands, depth, inputs), jnp.bfloat16),
        in_specs=[pl.BlockSpec(memory_space=pltpu.SMEM)] + [pl.BlockSpec(memory_space=pltpu.VMEM)] * phases,
        out_specs=pl.BlockSpec(memory_space=pltpu.VMEM),
        scratch_shapes=[
            pltpu.VMEM((phases, radix, rows, inputs), jnp.bfloat16),
            pltpu.SemaphoreType.DMA((phases,)),
        ],
        cost_estimate=pl.CostEstimate(flops=0, transcendentals=0, bytes_accessed=6 * bands * depth * inputs),
        name="bands",
    )(me.reshape(1), *blocks)


def left_kernel(near, right_ref, left_ref):
    for c in range(left_ref.shape[1]):
        turned = right_ref[c].astype(jnp.float32).T
        left_ref[0, c] = turned.astype(jnp.bfloat16)
        depth = turned.shape[1]
        real = lax.broadcasted_iota(jnp.int32, turned.shape, 1) % (2 * near) < near
        ahead = pltpu.roll(turned, depth - near, 1)
        behind = pltpu.roll(turned, near, 1)
        left_ref[1, c] = jnp.where(real, ahead, -behind).astype(jnp.bfloat16)


def left_of(right, near):
    bands, depth, inputs = right.shape
    return pl.pallas_call(
        functools.partial(left_kernel, near),
        out_shape=pltpu.VMEM((2, bands, inputs, depth), jnp.bfloat16),
        in_specs=[pl.BlockSpec(memory_space=pltpu.VMEM)],
        out_specs=pl.BlockSpec(memory_space=pltpu.VMEM),
        cost_estimate=pl.CostEstimate(flops=0, transcendentals=0, bytes_accessed=6 * bands * depth * inputs),
        name="left",
    )(right)


def correlate_kernel(near, group, jobs, scaling, me_ref, *rest):
    out_ref, buffer, sems = rest[-3:]
    halves = sorted({job[0] for job in jobs})
    lefts, rights = dict(zip(halves, rest)), rest[len(halves) :]
    slots, block, _, _, width = buffer.shape
    bands, depth = rest[0].shape[1], rest[0].shape[3]
    subs = near // group
    pieces = subs // block
    count = bands * pieces
    lanes = lax.broadcasted_iota(jnp.int32, (16, depth), 1) % near // group
    stations = out_ref.shape[-1] // width

    for at, (half, back) in enumerate(jobs):
        source = lax.rem(me_ref[0] + (stations - back), stations)
        columns = pl.ds(pl.multiple_of(source * width, width), width)

        def store(band, piece, slot):
            to = out_ref.at[band, pl.ds(half * subs + piece * block, block), :, :, columns]
            return pltpu.make_async_copy(buffer.at[slot], to, sems.at[slot])

        def item(i, _):
            band, piece, slot = i // pieces, i % pieces, (at * count + i) % slots

            @pl.when(at * count + i >= slots)
            def _():
                store(0, 0, slot).wait()

            right = rights[at][band]
            for k in range(block):
                mask = (lanes == piece * block + k).astype(jnp.float32).astype(jnp.bfloat16)[:1]
                for part in range(2):
                    product = jnp.dot(lefts[half][part, band] * mask, right, preferred_element_type=jnp.float32)
                    buffer[slot, k, part] = product * scaling
            store(band, piece, slot).start()
            return 0

        lax.fori_loop(0, count, item, 0)
    for slot in range(slots):
        store(0, 0, slot).wait()


def correlate(lefts, jobs, me, total, near, radix, scaling, shape):
    _, bands, inputs, depth = lefts[0].shape
    needed = [lefts[half] for half in sorted({job[0] for job in jobs})]
    group = AVG // radix
    block = math.gcd(near // group, 2)
    fresh = total is None
    flat = [array for _, _, array in jobs]
    listed = tuple((half, back) for half, back, _ in jobs)
    return pl.pallas_call(
        functools.partial(correlate_kernel, near, group, listed, scaling),
        out_shape=jax.ShapeDtypeStruct(shape, jnp.float32),
        in_specs=[pl.BlockSpec(memory_space=pltpu.SMEM)]
        + [pl.BlockSpec(memory_space=pltpu.VMEM)] * (len(needed) + len(flat))
        + ([] if fresh else [pl.BlockSpec(memory_space=pl.ANY)]),
        out_specs=pl.BlockSpec(memory_space=pl.ANY),
        scratch_shapes=[
            pltpu.VMEM((SLOTS_OUT, block, 2, inputs, inputs), jnp.float32),
            pltpu.SemaphoreType.DMA((SLOTS_OUT,)),
        ],
        input_output_aliases={} if fresh else {1 + len(needed) + len(flat): 0},
        cost_estimate=pl.CostEstimate(
            flops=4 * len(jobs) * bands * near // group * inputs * inputs * depth,
            transcendentals=0,
            bytes_accessed=8 * len(jobs) * bands * near // group * inputs * inputs,
        ),
        name="correlate",
    )(*([me.reshape(1)] + needed + flat + ([] if fresh else [total])))


def near_memory(array):
    return pltpu.with_memory_space_constraint(array, pltpu.VMEM)


def one_frame(voltages, fir_taps):
    inputs, _, _, slots = voltages.shape
    phases = fir_taps.shape[0]
    dests = lax.axis_size("chan")
    radix = slots // LANES
    near = LANES // dests // HALVES
    place = lax.axis_index("chan")
    branch = branch_of(voltages, fir_taps, place, dests)
    own, lefts = [], []
    for h in range(HALVES):
        blocks = list(branch[h])
        for k in range(1, dests):
            route = [(i, i ^ k) for i in range(dests)]
            blocks[k] = near_memory(lax.ppermute(blocks[k], "chan", route))
        own.append(near_memory(bands_of(blocks, place)))
        lefts.append(near_memory(left_of(own[h], near)))
    me = lax.axis_index("stn")
    stations = lax.axis_size("stn")
    shape = (phases // 2, HALVES * near * radix // AVG, 2, inputs, inputs * stations)
    scaling = 1.0 / (phases * slots * AVG)
    add = functools.partial(correlate, lefts, me=me, near=near, radix=radix, scaling=scaling, shape=shape)
    onward = [(i, (i + 1) % stations) for i in range(stations)]
    backward = [(i, (i - 1) % stations) for i in range(stations)]
    first, last, second = [], [], []
    for h, x in enumerate(own):
        first.append(near_memory(lax.ppermute(x, "stn", onward)))
        last.append(near_memory(lax.ppermute(x, "stn", backward)))
        second.append(near_memory(lax.ppermute(first[h], "stn", onward)))
    total = add([(0, 0, own[0])], total=None)
    total = add([(1, 0, own[1]), (0, 1, first[0]), (0, 3, last[0])], total=total)
    total = add([(0, 2, second[0]), (1, 1, first[1])], total=total)
    total = add([(1, 3, last[1])], total=total)
    total = add([(1, 2, second[1])], total=total)
    return total


def per_device(voltages, fir_taps):
    inputs, _, frames, slots = voltages.shape
    phases, tap_count, _ = fir_taps.shape
    lanes = lax.axis_size("chan")
    radix = slots // LANES
    fits = (
        lanes == phases
        and frames == tap_count
        and phases & (phases - 1) == 0
        and phases % 2 == 0
        and slots % LANES == 0
        and radix % 2 == 0
        and AVG % radix == 0
        and LANES % (8 * HALVES * lanes) == 0
        and lax.axis_size("stn") == 4
        and inputs % LANES == 0
    )
    return one_frame(voltages, fir_taps) if fits else all_frames(voltages, fir_taps)


def solution(mesh):
    return jax.shard_map(
        per_device,
        mesh=mesh,
        in_specs=(P("stn", "chan", None, None), P()),
        out_specs=P(None, "chan", None, "stn", None),
        check_vma=False,
    )
```

```python
import functools
import math

import jax
import jax.numpy as jnp
import numpy as np
from jax import lax
from jax.experimental import pallas as pl
from jax.experimental.pallas import tpu as pltpu
from jax.sharding import PartitionSpec as P

AVG = 16
LANES = 128
HALVES = 2
SLOTS_OUT = 4


def shifted(block, axis, distance):
    devices = range(lax.axis_size(axis))
    route = [(i - distance, i) for i in devices if i - distance in devices]
    return lax.ppermute(block, axis, route)


def rotation(numbers, modulus):
    angles = (numbers % modulus).astype(jnp.float32) * jnp.float32(-2.0 * math.pi / modulus)
    return (jnp.cos(angles), jnp.sin(angles))


def split_pair(table):
    upper = table.astype(jnp.bfloat16)
    lower = (table - upper.astype(jnp.float32)).astype(jnp.bfloat16)
    return (upper, lower)


def complex_table(real_part, imag_part, axis_at):
    first = jnp.stack([real_part, imag_part], axis=-1)
    second = jnp.stack([-imag_part, real_part], axis=-1)
    return jnp.stack([first, second], axis=axis_at)


def all_frames(voltages, fir_taps):
    inputs_dev, _, frames_dev, slot_count = voltages.shape
    phases = fir_taps.shape[0]
    tap_count = fir_taps.shape[1]
    lane_count = lax.axis_size("chan")
    groups = lane_count // phases
    position = lax.axis_index("chan")
    my_phase = position % phases
    my_group = position // phases
    recent = voltages[:, 0]
    if groups > 1:
        earlier = shifted(voltages[:, 0, frames_dev - (tap_count - 1) :, :], "chan", phases)
    else:
        earlier = jnp.zeros((inputs_dev, tap_count - 1, slot_count), voltages.dtype)
    series = jnp.concatenate([earlier, recent], axis=1)
    coeffs = lax.dynamic_index_in_dim(fir_taps, my_phase, 0, keepdims=False)
    frame_ids = my_group * frames_dev + jnp.arange(frames_dev, dtype=jnp.int32)
    keep_mask = (frame_ids >= tap_count - 1).astype(jnp.float32)
    filtered = sum(
        (
            coeffs[tap_index]
            * series[:, tap_count - 1 - tap_index : tap_count - 1 - tap_index + frames_dev].astype(
                jnp.float32
            )
            for tap_index in range(tap_count)
        )
    )
    filtered = filtered * keep_mask[None, :, None]
    better = lax.Precision.HIGH
    split_len = slot_count // phases
    folded = filtered.reshape(inputs_dev, frames_dev, split_len, phases)
    slot_ids = jnp.arange(split_len, dtype=jnp.int32)
    short_re, short_im = rotation(slot_ids[:, None] * slot_ids[None, :], split_len)
    short_table = jnp.stack([short_re, short_im], axis=-1)
    inner = jnp.einsum(
        "ifqr,qvc->rvcfi", folded, short_table, precision=better, preferred_element_type=jnp.float32
    )
    rest_ids = jnp.arange(phases, dtype=jnp.int32)
    freq_ids = jnp.arange(slot_count, dtype=jnp.int32).reshape(phases, split_len)
    twist_re, twist_im = rotation(
        (my_phase + phases * rest_ids)[:, None, None] * freq_ids[None], phases * slot_count
    )
    twist_table = complex_table(twist_re, twist_im, 3)
    branch = jnp.einsum(
        "rvcfi,ruvcd->uvfdi",
        inner,
        twist_table,
        precision=better,
        preferred_element_type=jnp.float32,
    )
    branch = branch.reshape(slot_count, 1, frames_dev, 2, inputs_dev).astype(jnp.bfloat16)
    band_count = phases // 2
    band_re, band_im = rotation(
        rest_ids[:, None] * jnp.arange(band_count, dtype=jnp.int32)[None, :], phases
    )
    band_table = complex_table(band_re, band_im, 1)
    band_upper, band_lower = split_pair(band_table)
    turned = lax.all_to_all(branch, "chan", split_axis=0, concat_axis=1, tiled=True)
    span_len = turned.shape[0]
    sources = turned.shape[1]
    item_count = turned.shape[2]
    grouped = turned.reshape(span_len, sources // phases, phases, item_count, 2, inputs_dev)
    phase_form = "wgpfci,pcbd->bwgfdi"
    total = jnp.einsum(
        phase_form, grouped, band_upper, preferred_element_type=jnp.float32
    ) + jnp.einsum(phase_form, grouped, band_lower, preferred_element_type=jnp.float32)
    spectra = total.astype(jnp.bfloat16)
    span_dev = spectra.shape[1]
    subs_dev = span_dev // AVG
    stacked = spectra.reshape(band_count, subs_dev, AVG * groups * frames_dev, 2, inputs_dev)
    columns = stacked.reshape(band_count, subs_dev, -1, inputs_dev)
    swapped = jnp.stack([stacked[:, :, :, 1], -stacked[:, :, :, 0]], axis=3).reshape(
        band_count, subs_dev, -1, inputs_dev
    )
    left_side = jnp.stack([columns, swapped], axis=2)
    spectra_count = groups * frames_dev - (tap_count - 1)
    scaling = 1.0 / (phases * slot_count * AVG * spectra_count)
    vis_form = "bsokn,bskw->bsonw"
    return (
        jnp.einsum(
            vis_form,
            left_side,
            lax.all_gather(columns, "stn", axis=3, tiled=True),
            preferred_element_type=jnp.float32,
        )
        * scaling
    )


def split_value(value):
    upper = value.astype(jnp.bfloat16)
    lower = (value - upper.astype(jnp.float32)).astype(jnp.bfloat16)
    return upper, lower


def weighted(terms, weights):
    total = None
    for term, weight in zip(terms, weights):
        if abs(weight) < 1e-9:
            continue
        part = term if abs(abs(weight) - 1.0) < 1e-9 else term * jnp.float32(abs(weight))
        if total is None:
            total = -part if weight < 0 else part
        else:
            total = total - part if weight < 0 else total + part
    return total


def turn_weights(count, step, radix):
    angles = [-2.0 * math.pi * ((k * step) % radix) / radix for k in range(count)]
    return [math.cos(a) for a in angles], [math.sin(a) for a in angles]


def half_sums(pieces):
    half = len(pieces) // 2
    sums = [pieces[k] + pieces[k + half] for k in range(half)]
    differences = [pieces[k] - pieces[k + half] for k in range(half)]
    return sums, differences


def branch_tables(phases, radix, dests):
    slots = radix * LANES
    near = LANES // dests
    rows = near // HALVES
    entry = np.arange(LANES).reshape(dests, HALVES, rows).transpose(1, 0, 2)
    v = np.repeat(entry[:, :, None], 2, axis=2).reshape(-1, 1)
    is_imag = np.broadcast_to(np.arange(2)[:, None], (HALVES, dests, 2, rows)).reshape(-1, 1)
    column = np.arange(2 * LANES)[None, :]
    b, half = column % LANES, column // LANES
    angle = -2.0 * np.pi * ((v * b) % LANES) / LANES + 0.5 * np.pi * (half - is_imag)
    far = np.stack([np.cos(angle), np.sin(angle)])
    phase = np.arange(phases)
    angle = -2.0 * np.pi * ((v * phase[None, :]) % slots) / slots
    row = np.stack([np.cos(angle), np.sin(angle)], axis=1).transpose(2, 0, 1)
    row = np.broadcast_to(row[..., None], row.shape + (1,))
    u = np.arange(radix)[None, :, None]
    turns = (u * (phase[:, None, None] + phases * b[None])) % (phases * slots)
    angle = -2.0 * np.pi * turns / (phases * slots)
    low = np.stack([np.cos(angle), np.sin(angle)], axis=1)
    mirrored = (u > radix // 2) & (half[None] == 1)
    low = np.where(mirrored[:, None], -low, low)
    return far.astype(np.float32), row[..., 0].astype(np.float32), low.astype(np.float32)


def table_copies(half, me, far_ref, row_ref, low_ref, far, row, low, sems):
    rows = pl.ds(half * far.shape[1], far.shape[1])
    pairs = ((far_ref.at[:, rows], far), (row_ref.at[me, rows], row), (low_ref.at[me], low))
    return [pltpu.make_async_copy(source, target, sems.at[i]) for i, (source, target) in enumerate(pairs)]


def make_table(me, dests, far, row, low, table):
    share = far.shape[1] // dests
    for k in range(dests):
        at = pl.ds(pl.multiple_of(lax.bitwise_xor(me, k) * share, share), share)
        row_cos, row_sin = row[at, 0:1], row[at, 1:2]
        far_cos = far[0, at] * row_cos - far[1, at] * row_sin
        far_sin = far[0, at] * row_sin + far[1, at] * row_cos
        for u in range(table.shape[1]):
            entry = far_cos * low[0, u : u + 1] - far_sin * low[1, u : u + 1]
            to = pl.ds(k * share, share)
            table[0, u, to], table[1, u, to] = split_value(entry)


def transform(table, y, outs):
    radix = table.shape[1]
    share = table.shape[2] // len(outs)
    for u in range(radix):
        source = min(u, radix - u)
        total = jnp.dot(table[0, u], y[source, 0], preferred_element_type=jnp.float32)
        total += jnp.dot(table[0, u], y[source, 1], preferred_element_type=jnp.float32)
        total += jnp.dot(table[1, u], y[source, 0], preferred_element_type=jnp.float32)
        total = total.astype(jnp.bfloat16)
        for k, out_ref in enumerate(outs):
            out_ref[u] = total[k * share : (k + 1) * share]


def first_kernel(radix, dests, place_ref, volt_ref, taps_ref, far_ref, row_ref, low_ref, *rest):
    outs = rest[:dests]
    y, volts, products, filtered, table, taps, far, row, low, volt_sems, sems = rest[dests:]
    me = place_ref[0]
    parts, rows = volts.shape[0], volts.shape[1]
    small = table_copies(0, me, far_ref, row_ref, low_ref, far, row, low, sems)
    small.append(pltpu.make_async_copy(taps_ref.at[me], taps, sems.at[3]))
    loads = [
        pltpu.make_async_copy(volt_ref.at[pl.ds(i * rows, rows), 0], volts.at[i], volt_sems.at[i])
        for i in range(parts)
    ]
    for load in small + loads:
        load.start()
    for load in small:
        load.wait()
    make_table(me, dests, far, row, low, table)
    by_frame = jnp.concatenate([taps[k : k + 1] for k in reversed(range(taps.shape[0]))], axis=0)
    together = LANES // rows
    for i, load in enumerate(loads):
        load.wait()
        frames = volts.shape[2]
        product = volts[i].astype(jnp.float32) * by_frame[None]
        for a in range(radix):
            columns = slice(a * LANES, (a + 1) * LANES)
            products[i % 2, a] = product[:, :, columns].reshape(rows * frames, LANES)
            terms = [products[i % 2, a, pl.ds(f, rows, stride=frames)] for f in range(frames)]
            filtered[pl.ds(i * rows, rows), columns] = sum(terms)
        if (i + 1) % together:
            continue
        inputs = pl.ds((i + 1) * rows - LANES, LANES)
        pieces = [filtered[inputs, a * LANES : (a + 1) * LANES].T for a in range(radix)]
        sums, differences = half_sums(pieces)
        for u in range(radix // 2 + 1):
            terms = differences if u % 2 else sums
            for part, weights in enumerate(turn_weights(radix // 2, u, radix)):
                value = weighted(terms, weights)
                if value is None:
                    value = jnp.zeros_like(pieces[0])
                at = (pl.ds(part * LANES, LANES), inputs)
                y[(u, 0) + at], y[(u, 1) + at] = split_value(value)
    transform(table, y, outs)


def next_kernel(half, dests, place_ref, y, far_ref, row_ref, low_ref, *rest):
    outs = rest[:dests]
    table, far, row, low, sems = rest[dests:]
    me = place_ref[0]
    small = table_copies(half, me, far_ref, row_ref, low_ref, far, row, low, sems)
    for load in small:
        load.start()
    for load in small:
        load.wait()
    make_table(me, dests, far, row, low, table)
    transform(table, y, outs)


def branch_of(voltages, fir_taps, me, dests):
    inputs, _, frames, slots = voltages.shape
    phases, tap_count, _ = fir_taps.shape
    radix = slots // LANES
    rows = LANES // dests // HALVES
    far, row, low = branch_tables(phases, radix, dests)
    parts = 8
    here = far.shape[1] // HALVES
    whole, near = pl.BlockSpec(memory_space=pl.ANY), pl.BlockSpec(memory_space=pltpu.VMEM)
    place = pl.BlockSpec(memory_space=pltpu.SMEM)
    blocks = [pltpu.VMEM((radix, 2 * rows, inputs), jnp.bfloat16)] * dests
    y = pltpu.VMEM((radix // 2 + 1, 2, 2 * LANES, inputs), jnp.bfloat16)
    table = pltpu.VMEM((2, radix, here, 2 * LANES), jnp.bfloat16)
    small = [
        pltpu.VMEM((2, here, 2 * LANES), jnp.float32),
        pltpu.VMEM((here, row.shape[2]), jnp.float32),
        pltpu.VMEM(low.shape[1:], jnp.float32),
    ]
    flops = 6 * radix * inputs * 2 * LANES * here
    *first, y = pl.pallas_call(
        functools.partial(first_kernel, radix, dests),
        out_shape=blocks + [y],
        in_specs=[place] + [whole] * 5,
        out_specs=[near] * (dests + 1),
        scratch_shapes=[
            pltpu.VMEM((parts, inputs // parts, frames, slots), jnp.bfloat16),
            pltpu.VMEM((2, radix, inputs // parts * frames, LANES), jnp.float32),
            pltpu.VMEM((inputs, slots), jnp.float32),
            table,
            pltpu.VMEM((tap_count, slots), jnp.float32),
        ]
        + small
        + [pltpu.SemaphoreType.DMA((parts,)), pltpu.SemaphoreType.DMA((4,))],
        cost_estimate=pl.CostEstimate(flops=flops, transcendentals=0, bytes_accessed=2 * voltages.size),
        name="branch",
    )(me.reshape(1), voltages, fir_taps, far, row, low)
    y = near_memory(y)
    result = [first]
    for half in range(1, HALVES):
        result.append(
            pl.pallas_call(
                functools.partial(next_kernel, half, dests),
                out_shape=blocks,
                in_specs=[place, near] + [whole] * 3,
                out_specs=[near] * dests,
                scratch_shapes=[table] + small + [pltpu.SemaphoreType.DMA((3,))],
                cost_estimate=pl.CostEstimate(flops=flops, transcendentals=0, bytes_accessed=4 * far.size),
                name="branch_next",
            )(me.reshape(1), y, far, row, low)
        )
    return [[near_memory(x) for x in part] for part in result]


def swapped(flag, low, high):
    return jnp.where(flag, high, low), jnp.where(flag, low, high)


def in_order(pieces, me, bit=0):
    step = 1 << bit
    if step == len(pieces):
        return pieces
    pieces = list(pieces)
    flag = lax.bitwise_and(me, step) != 0
    for k in range(len(pieces)):
        if not k & step:
            pieces[k], pieces[k + step] = swapped(flag, pieces[k], pieces[k + step])
    return in_order(pieces, me, bit + 1)


def band_kernel(place_ref, *rest):
    blocks, out_ref = rest[:-1], rest[-1]
    phases = len(blocks)
    radix, rows, _ = blocks[0].shape
    near, half = rows // 2, phases // 2
    me = place_ref[0]
    sign = jnp.where(lax.bitwise_and(me, half) != 0, -1.0, 1.0).astype(jnp.float32)
    for u in range(radix):
        full = [block[u].astype(jnp.float32) for block in blocks]
        sums, differences = half_sums(full)
        pair = [in_order(sums, me), in_order([d * sign for d in differences], me)]
        for c in range(half):
            cos_w, sin_w = turn_weights(half, c, phases)
            terms = [x[:near] for x in pair[c % 2]] + [x[near:] for x in pair[c % 2]]
            spectrum = [weighted(terms, cos_w + [-w for w in sin_w]), weighted(terms, sin_w + cos_w)]
            out_ref[c, u * rows : (u + 1) * rows] = jnp.concatenate(spectrum, axis=0).astype(jnp.bfloat16)


def bands_of(blocks, me):
    phases = len(blocks)
    radix, rows, inputs = blocks[0].shape
    bands, depth = phases // 2, radix * rows
    return pl.pallas_call(
        band_kernel,
        out_shape=pltpu.VMEM((bands, depth, inputs), jnp.bfloat16),
        in_specs=[pl.BlockSpec(memory_space=pltpu.SMEM)] + [pl.BlockSpec(memory_space=pltpu.VMEM)] * phases,
        out_specs=pl.BlockSpec(memory_space=pltpu.VMEM),
        cost_estimate=pl.CostEstimate(flops=0, transcendentals=0, bytes_accessed=6 * bands * depth * inputs),
        name="bands",
    )(me.reshape(1), *blocks)


def left_kernel(near, right_ref, left_ref):
    for c in range(left_ref.shape[1]):
        turned = right_ref[c].astype(jnp.float32).T
        left_ref[0, c] = turned.astype(jnp.bfloat16)
        depth = turned.shape[1]
        real = lax.broadcasted_iota(jnp.int32, turned.shape, 1) % (2 * near) < near
        ahead = pltpu.roll(turned, depth - near, 1)
        behind = pltpu.roll(turned, near, 1)
        left_ref[1, c] = jnp.where(real, ahead, -behind).astype(jnp.bfloat16)


def left_of(right, near):
    bands, depth, inputs = right.shape
    return pl.pallas_call(
        functools.partial(left_kernel, near),
        out_shape=pltpu.VMEM((2, bands, inputs, depth), jnp.bfloat16),
        in_specs=[pl.BlockSpec(memory_space=pltpu.VMEM)],
        out_specs=pl.BlockSpec(memory_space=pltpu.VMEM),
        cost_estimate=pl.CostEstimate(flops=0, transcendentals=0, bytes_accessed=6 * bands * depth * inputs),
        name="left",
    )(right)


def correlate_kernel(near, group, jobs, scaling, me_ref, *rest):
    out_ref, buffer, sems = rest[-3:]
    halves = sorted({job[0] for job in jobs})
    lefts, rights = dict(zip(halves, rest)), rest[len(halves) :]
    slots, block, _, _, width = buffer.shape
    bands, depth = rest[0].shape[1], rest[0].shape[3]
    subs = near // group
    pieces = subs // block
    count = bands * pieces
    lanes = lax.broadcasted_iota(jnp.int32, (16, depth), 1) % near // group
    stations = out_ref.shape[-1] // width

    for at, (half, back) in enumerate(jobs):
        source = lax.rem(me_ref[0] + (stations - back), stations)
        columns = pl.ds(pl.multiple_of(source * width, width), width)

        def store(band, piece, slot):
            to = out_ref.at[band, pl.ds(half * subs + piece * block, block), :, :, columns]
            return pltpu.make_async_copy(buffer.at[slot], to, sems.at[slot])

        def item(i, _):
            band, piece, slot = i // pieces, i % pieces, (at * count + i) % slots

            @pl.when(at * count + i >= slots)
            def _():
                store(0, 0, slot).wait()

            right = rights[at][band]
            for k in range(block):
                mask = (lanes == piece * block + k).astype(jnp.float32).astype(jnp.bfloat16)[:1]
                for part in range(2):
                    product = jnp.dot(lefts[half][part, band] * mask, right, preferred_element_type=jnp.float32)
                    buffer[slot, k, part] = product * scaling
            store(band, piece, slot).start()
            return 0

        lax.fori_loop(0, count, item, 0)
    for slot in range(slots):
        store(0, 0, slot).wait()


def correlate(lefts, jobs, me, total, near, radix, scaling, shape):
    _, bands, inputs, depth = lefts[0].shape
    needed = [lefts[half] for half in sorted({job[0] for job in jobs})]
    group = AVG // radix
    block = math.gcd(near // group, 2)
    fresh = total is None
    flat = [array for _, _, array in jobs]
    listed = tuple((half, back) for half, back, _ in jobs)
    return pl.pallas_call(
        functools.partial(correlate_kernel, near, group, listed, scaling),
        out_shape=jax.ShapeDtypeStruct(shape, jnp.float32),
        in_specs=[pl.BlockSpec(memory_space=pltpu.SMEM)]
        + [pl.BlockSpec(memory_space=pltpu.VMEM)] * (len(needed) + len(flat))
        + ([] if fresh else [pl.BlockSpec(memory_space=pl.ANY)]),
        out_specs=pl.BlockSpec(memory_space=pl.ANY),
        scratch_shapes=[
            pltpu.VMEM((SLOTS_OUT, block, 2, inputs, inputs), jnp.float32),
            pltpu.SemaphoreType.DMA((SLOTS_OUT,)),
        ],
        input_output_aliases={} if fresh else {1 + len(needed) + len(flat): 0},
        cost_estimate=pl.CostEstimate(
            flops=4 * len(jobs) * bands * near // group * inputs * inputs * depth,
            transcendentals=0,
            bytes_accessed=8 * len(jobs) * bands * near // group * inputs * inputs,
        ),
        name="correlate",
    )(*([me.reshape(1)] + needed + flat + ([] if fresh else [total])))


def near_memory(array):
    return pltpu.with_memory_space_constraint(array, pltpu.VMEM)


def one_frame(voltages, fir_taps):
    inputs, _, _, slots = voltages.shape
    phases = fir_taps.shape[0]
    dests = lax.axis_size("chan")
    radix = slots // LANES
    near = LANES // dests // HALVES
    place = lax.axis_index("chan")
    branch = branch_of(voltages, fir_taps, place, dests)
    own, lefts = [], []
    for h in range(HALVES):
        blocks = list(branch[h])
        for k in range(1, dests):
            route = [(i, i ^ k) for i in range(dests)]
            blocks[k] = near_memory(lax.ppermute(blocks[k], "chan", route))
        own.append(near_memory(bands_of(blocks, place)))
        lefts.append(near_memory(left_of(own[h], near)))
    me = lax.axis_index("stn")
    stations = lax.axis_size("stn")
    shape = (phases // 2, HALVES * near * radix // AVG, 2, inputs, inputs * stations)
    scaling = 1.0 / (phases * slots * AVG)
    add = functools.partial(correlate, lefts, me=me, near=near, radix=radix, scaling=scaling, shape=shape)
    onward = [(i, (i + 1) % stations) for i in range(stations)]
    backward = [(i, (i - 1) % stations) for i in range(stations)]
    first, last, second = [], [], []
    for h, x in enumerate(own):
        first.append(near_memory(lax.ppermute(x, "stn", onward)))
        last.append(near_memory(lax.ppermute(x, "stn", backward)))
        second.append(near_memory(lax.ppermute(first[h], "stn", onward)))
    total = add([(0, 0, own[0])], total=None)
    total = add([(1, 0, own[1]), (0, 1, first[0]), (0, 3, last[0])], total=total)
    total = add([(0, 2, second[0]), (1, 1, first[1])], total=total)
    total = add([(1, 3, last[1])], total=total)
    total = add([(1, 2, second[1])], total=total)
    return total


def per_device(voltages, fir_taps):
    inputs, _, frames, slots = voltages.shape
    phases, tap_count, _ = fir_taps.shape
    lanes = lax.axis_size("chan")
    radix = slots // LANES
    fits = (
        lanes == phases
        and frames == tap_count
        and phases & (phases - 1) == 0
        and phases % 2 == 0
        and slots % LANES == 0
        and radix % 2 == 0
        and AVG % radix == 0
        and LANES % (8 * HALVES * lanes) == 0
        and lax.axis_size("stn") == 4
        and inputs % LANES == 0
    )
    return one_frame(voltages, fir_taps) if fits else all_frames(voltages, fir_taps)


def solution(mesh):
    return jax.shard_map(
        per_device,
        mesh=mesh,
        in_specs=(P("stn", "chan", None, None), P()),
        out_specs=P(None, "chan", None, "stn", None),
        check_vma=False,
    )
```

```python
import functools
import math

import jax
import jax.numpy as jnp
import numpy as np
from jax import lax
from jax.experimental import pallas as pl
from jax.experimental.pallas import tpu as pltpu
from jax.sharding import PartitionSpec as P

AVG = 16
LANES = 128
HALVES = 2
SLOTS_OUT = 4


def shifted(block, axis, distance):
    devices = range(lax.axis_size(axis))
    route = [(i - distance, i) for i in devices if i - distance in devices]
    return lax.ppermute(block, axis, route)


def rotation(numbers, modulus):
    angles = (numbers % modulus).astype(jnp.float32) * jnp.float32(-2.0 * math.pi / modulus)
    return (jnp.cos(angles), jnp.sin(angles))


def split_pair(table):
    upper = table.astype(jnp.bfloat16)
    lower = (table - upper.astype(jnp.float32)).astype(jnp.bfloat16)
    return (upper, lower)


def complex_table(real_part, imag_part, axis_at):
    first = jnp.stack([real_part, imag_part], axis=-1)
    second = jnp.stack([-imag_part, real_part], axis=-1)
    return jnp.stack([first, second], axis=axis_at)


def all_frames(voltages, fir_taps):
    inputs_dev, _, frames_dev, slot_count = voltages.shape
    phases = fir_taps.shape[0]
    tap_count = fir_taps.shape[1]
    lane_count = lax.axis_size("chan")
    groups = lane_count // phases
    position = lax.axis_index("chan")
    my_phase = position % phases
    my_group = position // phases
    recent = voltages[:, 0]
    if groups > 1:
        earlier = shifted(voltages[:, 0, frames_dev - (tap_count - 1) :, :], "chan", phases)
    else:
        earlier = jnp.zeros((inputs_dev, tap_count - 1, slot_count), voltages.dtype)
    series = jnp.concatenate([earlier, recent], axis=1)
    coeffs = lax.dynamic_index_in_dim(fir_taps, my_phase, 0, keepdims=False)
    frame_ids = my_group * frames_dev + jnp.arange(frames_dev, dtype=jnp.int32)
    keep_mask = (frame_ids >= tap_count - 1).astype(jnp.float32)
    filtered = sum(
        (
            coeffs[tap_index]
            * series[:, tap_count - 1 - tap_index : tap_count - 1 - tap_index + frames_dev].astype(
                jnp.float32
            )
            for tap_index in range(tap_count)
        )
    )
    filtered = filtered * keep_mask[None, :, None]
    better = lax.Precision.HIGH
    split_len = slot_count // phases
    folded = filtered.reshape(inputs_dev, frames_dev, split_len, phases)
    slot_ids = jnp.arange(split_len, dtype=jnp.int32)
    short_re, short_im = rotation(slot_ids[:, None] * slot_ids[None, :], split_len)
    short_table = jnp.stack([short_re, short_im], axis=-1)
    inner = jnp.einsum(
        "ifqr,qvc->rvcfi", folded, short_table, precision=better, preferred_element_type=jnp.float32
    )
    rest_ids = jnp.arange(phases, dtype=jnp.int32)
    freq_ids = jnp.arange(slot_count, dtype=jnp.int32).reshape(phases, split_len)
    twist_re, twist_im = rotation(
        (my_phase + phases * rest_ids)[:, None, None] * freq_ids[None], phases * slot_count
    )
    twist_table = complex_table(twist_re, twist_im, 3)
    branch = jnp.einsum(
        "rvcfi,ruvcd->uvfdi",
        inner,
        twist_table,
        precision=better,
        preferred_element_type=jnp.float32,
    )
    branch = branch.reshape(slot_count, 1, frames_dev, 2, inputs_dev).astype(jnp.bfloat16)
    band_count = phases // 2
    band_re, band_im = rotation(
        rest_ids[:, None] * jnp.arange(band_count, dtype=jnp.int32)[None, :], phases
    )
    band_table = complex_table(band_re, band_im, 1)
    band_upper, band_lower = split_pair(band_table)
    turned = lax.all_to_all(branch, "chan", split_axis=0, concat_axis=1, tiled=True)
    span_len = turned.shape[0]
    sources = turned.shape[1]
    item_count = turned.shape[2]
    grouped = turned.reshape(span_len, sources // phases, phases, item_count, 2, inputs_dev)
    phase_form = "wgpfci,pcbd->bwgfdi"
    total = jnp.einsum(
        phase_form, grouped, band_upper, preferred_element_type=jnp.float32
    ) + jnp.einsum(phase_form, grouped, band_lower, preferred_element_type=jnp.float32)
    spectra = total.astype(jnp.bfloat16)
    span_dev = spectra.shape[1]
    subs_dev = span_dev // AVG
    stacked = spectra.reshape(band_count, subs_dev, AVG * groups * frames_dev, 2, inputs_dev)
    columns = stacked.reshape(band_count, subs_dev, -1, inputs_dev)
    swapped = jnp.stack([stacked[:, :, :, 1], -stacked[:, :, :, 0]], axis=3).reshape(
        band_count, subs_dev, -1, inputs_dev
    )
    left_side = jnp.stack([columns, swapped], axis=2)
    spectra_count = groups * frames_dev - (tap_count - 1)
    scaling = 1.0 / (phases * slot_count * AVG * spectra_count)
    vis_form = "bsokn,bskw->bsonw"
    return (
        jnp.einsum(
            vis_form,
            left_side,
            lax.all_gather(columns, "stn", axis=3, tiled=True),
            preferred_element_type=jnp.float32,
        )
        * scaling
    )


def split_value(value):
    upper = value.astype(jnp.bfloat16)
    lower = (value - upper.astype(jnp.float32)).astype(jnp.bfloat16)
    return upper, lower


def weighted(terms, weights):
    total = None
    for term, weight in zip(terms, weights):
        if abs(weight) < 1e-9:
            continue
        part = term if abs(abs(weight) - 1.0) < 1e-9 else term * jnp.float32(abs(weight))
        if total is None:
            total = -part if weight < 0 else part
        else:
            total = total - part if weight < 0 else total + part
    return total


def turn_weights(count, step, radix):
    angles = [-2.0 * math.pi * ((k * step) % radix) / radix for k in range(count)]
    return [math.cos(a) for a in angles], [math.sin(a) for a in angles]


def half_sums(pieces):
    half = len(pieces) // 2
    sums = [pieces[k] + pieces[k + half] for k in range(half)]
    differences = [pieces[k] - pieces[k + half] for k in range(half)]
    return sums, differences


def branch_tables(phases, radix, dests):
    slots = radix * LANES
    near = LANES // dests
    rows = near // HALVES
    entry = np.arange(LANES).reshape(dests, HALVES, rows).transpose(1, 0, 2)
    v = np.repeat(entry[:, :, None], 2, axis=2).reshape(-1, 1)
    is_imag = np.broadcast_to(np.arange(2)[:, None], (HALVES, dests, 2, rows)).reshape(-1, 1)
    column = np.arange(2 * LANES)[None, :]
    b, half = column % LANES, column // LANES
    angle = -2.0 * np.pi * ((v * b) % LANES) / LANES + 0.5 * np.pi * (half - is_imag)
    far = np.stack([np.cos(angle), np.sin(angle)])
    phase = np.arange(phases)
    angle = -2.0 * np.pi * ((v * phase[None, :]) % slots) / slots
    row = np.stack([np.cos(angle), np.sin(angle)], axis=1).transpose(2, 0, 1)
    row = np.broadcast_to(row[..., None], row.shape + (1,))
    u = np.arange(radix)[None, :, None]
    turns = (u * (phase[:, None, None] + phases * b[None])) % (phases * slots)
    angle = -2.0 * np.pi * turns / (phases * slots)
    low = np.stack([np.cos(angle), np.sin(angle)], axis=1)
    mirrored = (u > radix // 2) & (half[None] == 1)
    low = np.where(mirrored[:, None], -low, low)
    return far.astype(np.float32), row[..., 0].astype(np.float32), low.astype(np.float32)


def table_copies(half, me, far_ref, row_ref, low_ref, far, row, low, sems):
    rows = pl.ds(half * far.shape[1], far.shape[1])
    pairs = ((far_ref.at[:, rows], far), (row_ref.at[me, rows], row), (low_ref.at[me], low))
    return [pltpu.make_async_copy(source, target, sems.at[i]) for i, (source, target) in enumerate(pairs)]


def make_table(me, dests, far, row, low, table):
    share = far.shape[1] // dests
    for k in range(dests):
        at = pl.ds(pl.multiple_of(lax.bitwise_xor(me, k) * share, share), share)
        row_cos, row_sin = row[at, 0:1], row[at, 1:2]
        far_cos = far[0, at] * row_cos - far[1, at] * row_sin
        far_sin = far[0, at] * row_sin + far[1, at] * row_cos
        for u in range(table.shape[1]):
            entry = far_cos * low[0, u : u + 1] - far_sin * low[1, u : u + 1]
            to = pl.ds(k * share, share)
            table[0, u, to], table[1, u, to] = split_value(entry)


def transform(table, y, outs):
    radix = table.shape[1]
    share = table.shape[2] // len(outs)
    for u in range(radix):
        source = min(u, radix - u)
        total = jnp.dot(table[0, u], y[source, 0], preferred_element_type=jnp.float32)
        total += jnp.dot(table[0, u], y[source, 1], preferred_element_type=jnp.float32)
        total += jnp.dot(table[1, u], y[source, 0], preferred_element_type=jnp.float32)
        total = total.astype(jnp.bfloat16)
        for k, out_ref in enumerate(outs):
            out_ref[u] = total[k * share : (k + 1) * share]


def first_kernel(radix, dests, place_ref, volt_ref, taps_ref, far_ref, row_ref, low_ref, *rest):
    outs = rest[:dests]
    y, volts, products, filtered, table, taps, far, row, low, volt_sems, sems = rest[dests:]
    me = place_ref[0]
    parts, rows = volts.shape[0], volts.shape[1]
    small = table_copies(0, me, far_ref, row_ref, low_ref, far, row, low, sems)
    small.append(pltpu.make_async_copy(taps_ref.at[me], taps, sems.at[3]))
    loads = [
        pltpu.make_async_copy(volt_ref.at[pl.ds(i * rows, rows), 0], volts.at[i], volt_sems.at[i])
        for i in range(parts)
    ]
    for load in small + loads:
        load.start()
    for load in small:
        load.wait()
    make_table(me, dests, far, row, low, table)
    by_frame = jnp.concatenate([taps[k : k + 1] for k in reversed(range(taps.shape[0]))], axis=0)
    together = LANES // rows
    for i, load in enumerate(loads):
        load.wait()
        frames = volts.shape[2]
        product = volts[i].astype(jnp.float32) * by_frame[None]
        for a in range(radix):
            columns = slice(a * LANES, (a + 1) * LANES)
            products[i % 2, a] = product[:, :, columns].reshape(rows * frames, LANES)
            terms = [products[i % 2, a, pl.ds(f, rows, stride=frames)] for f in range(frames)]
            filtered[pl.ds(i * rows, rows), columns] = sum(terms)
        if (i + 1) % together:
            continue
        inputs = pl.ds((i + 1) * rows - LANES, LANES)
        pieces = [filtered[inputs, a * LANES : (a + 1) * LANES].T for a in range(radix)]
        sums, differences = half_sums(pieces)
        for u in range(radix // 2 + 1):
            terms = differences if u % 2 else sums
            for part, weights in enumerate(turn_weights(radix // 2, u, radix)):
                value = weighted(terms, weights)
                if value is None:
                    value = jnp.zeros_like(pieces[0])
                at = (pl.ds(part * LANES, LANES), inputs)
                y[(u, 0) + at], y[(u, 1) + at] = split_value(value)
    transform(table, y, outs)


def next_kernel(half, dests, place_ref, y, far_ref, row_ref, low_ref, *rest):
    keep, give, (table, far, row, low, sems) = rest[: dests // 2], rest[dests // 2], rest[dests // 2 + 1 :]
    outs = [keep[k // 2] if k % 2 == 0 else give.at[k // 2] for k in range(dests)]
    me = place_ref[0]
    small = table_copies(half, me, far_ref, row_ref, low_ref, far, row, low, sems)
    for load in small:
        load.start()
    for load in small:
        load.wait()
    make_table(me, dests, far, row, low, table)
    transform(table, y, outs)


def branch_of(voltages, fir_taps, me, dests):
    inputs, _, frames, slots = voltages.shape
    phases, tap_count, _ = fir_taps.shape
    radix = slots // LANES
    rows = LANES // dests // HALVES
    far, row, low = branch_tables(phases, radix, dests)
    parts = 16
    here = far.shape[1] // HALVES
    whole, near = pl.BlockSpec(memory_space=pl.ANY), pl.BlockSpec(memory_space=pltpu.VMEM)
    place = pl.BlockSpec(memory_space=pltpu.SMEM)
    blocks = [pltpu.VMEM((radix, 2 * rows, inputs), jnp.bfloat16)] * dests
    give = pltpu.VMEM((dests // 2, radix, 2 * rows, inputs), jnp.bfloat16)
    y = pltpu.VMEM((radix // 2 + 1, 2, 2 * LANES, inputs), jnp.bfloat16)
    table = pltpu.VMEM((2, radix, here, 2 * LANES), jnp.bfloat16)
    small = [
        pltpu.VMEM((2, here, 2 * LANES), jnp.float32),
        pltpu.VMEM((here, row.shape[2]), jnp.float32),
        pltpu.VMEM(low.shape[1:], jnp.float32),
    ]
    flops = 6 * radix * inputs * 2 * LANES * here
    *first, y = pl.pallas_call(
        functools.partial(first_kernel, radix, dests),
        out_shape=blocks + [y],
        in_specs=[place] + [whole] * 5,
        out_specs=[near] * (dests + 1),
        scratch_shapes=[
            pltpu.VMEM((parts, inputs // parts, frames, slots), jnp.bfloat16),
            pltpu.VMEM((2, radix, inputs // parts * frames, LANES), jnp.float32),
            pltpu.VMEM((inputs, slots), jnp.float32),
            table,
            pltpu.VMEM((tap_count, slots), jnp.float32),
        ]
        + small
        + [pltpu.SemaphoreType.DMA((parts,)), pltpu.SemaphoreType.DMA((4,))],
        cost_estimate=pl.CostEstimate(flops=flops, transcendentals=0, bytes_accessed=2 * voltages.size),
        name="branch",
    )(me.reshape(1), voltages, fir_taps, far, row, low)
    y = near_memory(y)
    result = [first]
    for half in range(1, HALVES):
        result.append(
            pl.pallas_call(
                functools.partial(next_kernel, half, dests),
                out_shape=blocks[: dests // 2] + [give],
                in_specs=[place, near] + [whole] * 3,
                out_specs=[near] * (dests // 2 + 1),
                scratch_shapes=[table] + small + [pltpu.SemaphoreType.DMA((3,))],
                cost_estimate=pl.CostEstimate(flops=flops, transcendentals=0, bytes_accessed=4 * far.size),
                name="branch_next",
            )(me.reshape(1), y, far, row, low)
        )
    return [[near_memory(x) for x in part] for part in result]


def swapped(flag, low, high):
    return jnp.where(flag, high, low), jnp.where(flag, low, high)


def in_order(pieces, me, bit=0):
    step = 1 << bit
    if step == len(pieces):
        return pieces
    pieces = list(pieces)
    flag = lax.bitwise_and(me, step) != 0
    for k in range(len(pieces)):
        if not k & step:
            pieces[k], pieces[k + step] = swapped(flag, pieces[k], pieces[k + step])
    return in_order(pieces, me, bit + 1)


def join_kernel(*refs):
    count = len(refs) // 2
    keep, got, outs = refs[:count], refs[count], refs[count + 1 :]
    for m, out_ref in enumerate(outs):
        out_ref[0] = keep[m][...]
        out_ref[1] = got[m + 1]


def join(keep, got):
    shape = keep[0].shape
    near = pl.BlockSpec(memory_space=pltpu.VMEM)
    return pl.pallas_call(
        join_kernel,
        out_shape=[pltpu.VMEM((2,) + shape, keep[0].dtype)] * len(keep),
        in_specs=[near] * (len(keep) + 1),
        out_specs=[near] * len(keep),
        name="join",
    )(*keep, got)


def band_kernel(place_ref, *rest):
    out_ref, blocks = rest[-1], []
    for ref in rest[:-1]:
        if len(ref.shape) == 3:
            blocks.append(ref)
        else:
            blocks += [ref.at[0]] if ref.shape[0] > 2 else [ref.at[0], ref.at[1]]
    phases = len(blocks)
    radix, rows, _ = blocks[0].shape
    near, half = rows // 2, phases // 2
    me = place_ref[0]
    sign = jnp.where(lax.bitwise_and(me, half) != 0, -1.0, 1.0).astype(jnp.float32)
    for u in range(radix):
        full = [block[u].astype(jnp.float32) for block in blocks]
        sums, differences = half_sums(full)
        pair = [in_order(sums, me), in_order([d * sign for d in differences], me)]
        for c in range(half):
            cos_w, sin_w = turn_weights(half, c, phases)
            terms = [x[:near] for x in pair[c % 2]] + [x[near:] for x in pair[c % 2]]
            spectrum = [weighted(terms, cos_w + [-w for w in sin_w]), weighted(terms, sin_w + cos_w)]
            out_ref[c, u * rows : (u + 1) * rows] = jnp.concatenate(spectrum, axis=0).astype(jnp.bfloat16)


def bands_of(blocks, me, phases):
    radix, rows, inputs = blocks[0].shape
    bands, depth = phases // 2, radix * rows
    return pl.pallas_call(
        band_kernel,
        out_shape=pltpu.VMEM((bands, depth, inputs), jnp.bfloat16),
        in_specs=[pl.BlockSpec(memory_space=pltpu.SMEM)] + [pl.BlockSpec(memory_space=pltpu.VMEM)] * len(blocks),
        out_specs=pl.BlockSpec(memory_space=pltpu.VMEM),
        cost_estimate=pl.CostEstimate(flops=0, transcendentals=0, bytes_accessed=6 * bands * depth * inputs),
        name="bands",
    )(me.reshape(1), *blocks)


def left_kernel(near, right_ref, left_ref):
    for c in range(left_ref.shape[1]):
        turned = right_ref[c].astype(jnp.float32).T
        left_ref[0, c] = turned.astype(jnp.bfloat16)
        depth = turned.shape[1]
        real = lax.broadcasted_iota(jnp.int32, turned.shape, 1) % (2 * near) < near
        ahead = pltpu.roll(turned, depth - near, 1)
        behind = pltpu.roll(turned, near, 1)
        left_ref[1, c] = jnp.where(real, ahead, -behind).astype(jnp.bfloat16)


def left_of(right, near):
    bands, depth, inputs = right.shape
    return pl.pallas_call(
        functools.partial(left_kernel, near),
        out_shape=pltpu.VMEM((2, bands, inputs, depth), jnp.bfloat16),
        in_specs=[pl.BlockSpec(memory_space=pltpu.VMEM)],
        out_specs=pl.BlockSpec(memory_space=pltpu.VMEM),
        cost_estimate=pl.CostEstimate(flops=0, transcendentals=0, bytes_accessed=6 * bands * depth * inputs),
        name="left",
    )(right)


def correlate_kernel(near, group, jobs, scaling, me_ref, *rest):
    out_ref, buffer, sems = rest[-3:]
    halves = sorted({job[0] for job in jobs})
    lefts, rights = dict(zip(halves, rest)), rest[len(halves) :]
    slots, block, _, _, width = buffer.shape
    bands, depth = rest[0].shape[1], rest[0].shape[3]
    subs = near // group
    pieces = subs // block
    count = bands * pieces
    lanes = lax.broadcasted_iota(jnp.int32, (16, depth), 1) % near // group
    stations = out_ref.shape[-1] // width

    for at, (half, back) in enumerate(jobs):
        source = lax.rem(me_ref[0] + (stations - back), stations)
        columns = pl.ds(pl.multiple_of(source * width, width), width)

        def store(band, piece, slot):
            to = out_ref.at[band, pl.ds(half * subs + piece * block, block), :, :, columns]
            return pltpu.make_async_copy(buffer.at[slot], to, sems.at[slot])

        def item(i, _):
            band, piece, slot = i // pieces, i % pieces, (at * count + i) % slots

            @pl.when(at * count + i >= slots)
            def _():
                store(0, 0, slot).wait()

            right = rights[at][band]
            for k in range(block):
                mask = (lanes == piece * block + k).astype(jnp.float32).astype(jnp.bfloat16)[:1]
                for part in range(2):
                    product = jnp.dot(lefts[half][part, band] * mask, right, preferred_element_type=jnp.float32)
                    buffer[slot, k, part] = product * scaling
            store(band, piece, slot).start()
            return 0

        lax.fori_loop(0, count, item, 0)
    for slot in range(slots):
        store(0, 0, slot).wait()


def correlate(lefts, jobs, me, total, near, radix, scaling, shape):
    _, bands, inputs, depth = lefts[0].shape
    needed = [lefts[half] for half in sorted({job[0] for job in jobs})]
    group = AVG // radix
    block = math.gcd(near // group, 2)
    fresh = total is None
    flat = [array for _, _, array in jobs]
    listed = tuple((half, back) for half, back, _ in jobs)
    return pl.pallas_call(
        functools.partial(correlate_kernel, near, group, listed, scaling),
        out_shape=jax.ShapeDtypeStruct(shape, jnp.float32),
        in_specs=[pl.BlockSpec(memory_space=pltpu.SMEM)]
        + [pl.BlockSpec(memory_space=pltpu.VMEM)] * (len(needed) + len(flat))
        + ([] if fresh else [pl.BlockSpec(memory_space=pl.ANY)]),
        out_specs=pl.BlockSpec(memory_space=pl.ANY),
        scratch_shapes=[
            pltpu.VMEM((SLOTS_OUT, block, 2, inputs, inputs), jnp.float32),
            pltpu.SemaphoreType.DMA((SLOTS_OUT,)),
        ],
        input_output_aliases={} if fresh else {1 + len(needed) + len(flat): 0},
        cost_estimate=pl.CostEstimate(
            flops=4 * len(jobs) * bands * near // group * inputs * inputs * depth,
            transcendentals=0,
            bytes_accessed=8 * len(jobs) * bands * near // group * inputs * inputs,
        ),
        name="correlate",
    )(*([me.reshape(1)] + needed + flat + ([] if fresh else [total])))


def near_memory(array):
    return pltpu.with_memory_space_constraint(array, pltpu.VMEM)


def one_frame(voltages, fir_taps):
    inputs, _, _, slots = voltages.shape
    phases = fir_taps.shape[0]
    dests = lax.axis_size("chan")
    radix = slots // LANES
    near = LANES // dests // HALVES
    place = lax.axis_index("chan")
    branch = branch_of(voltages, fir_taps, place, dests)
    own, lefts = [], []
    for h in range(HALVES):
        blocks = list(branch[h])
        if h > 0:
            keep, got = blocks[:-1], lax.ppermute(blocks[-1], "chan", [(i, i ^ 1) for i in range(dests)])
            got = near_memory(got)
            pairs = join(keep[1:], got)
            blocks = [keep[0], got] + [near_memory(x) for x in pairs]
        for at in range(1 if h == 0 else 2, len(blocks)):
            k = at if h == 0 else 2 * (at - 1)
            route = [(i, i ^ k) for i in range(dests)]
            blocks[at] = near_memory(lax.ppermute(blocks[at], "chan", route))
        own.append(near_memory(bands_of(blocks, place, phases)))
        lefts.append(near_memory(left_of(own[h], near)))
    me = lax.axis_index("stn")
    stations = lax.axis_size("stn")
    shape = (phases // 2, HALVES * near * radix // AVG, 2, inputs, inputs * stations)
    scaling = 1.0 / (phases * slots * AVG)
    add = functools.partial(correlate, lefts, me=me, near=near, radix=radix, scaling=scaling, shape=shape)
    onward = [(i, (i + 1) % stations) for i in range(stations)]
    backward = [(i, (i - 1) % stations) for i in range(stations)]
    first, last, second = [], [], []
    for h, x in enumerate(own):
        first.append(near_memory(lax.ppermute(x, "stn", onward)))
        last.append(near_memory(lax.ppermute(x, "stn", backward)))
        second.append(near_memory(lax.ppermute(first[h], "stn", onward)))
    jobs = (
        [(0, 0, own[0])],
        [(1, 0, own[1]), (0, 1, first[0])],
        [(0, 3, last[0]), (1, 1, first[1])],
        [(0, 2, second[0])],
        [(1, 3, last[1])],
        [(1, 2, second[1])],
    )
    total = None
    for job in jobs:
        total = add(job, total=total)
    return total


def per_device(voltages, fir_taps):
    inputs, _, frames, slots = voltages.shape
    phases, tap_count, _ = fir_taps.shape
    lanes = lax.axis_size("chan")
    radix = slots // LANES
    fits = (
        lanes == phases
        and frames == tap_count
        and phases & (phases - 1) == 0
        and phases > 4
        and slots % LANES == 0
        and radix % 2 == 0
        and AVG % radix == 0
        and LANES % (8 * HALVES * lanes) == 0
        and lax.axis_size("stn") == 4
        and inputs % LANES == 0
    )
    return one_frame(voltages, fir_taps) if fits else all_frames(voltages, fir_taps)


def solution(mesh):
    return jax.shard_map(
        per_device,
        mesh=mesh,
        in_specs=(P("stn", "chan", None, None), P()),
        out_specs=P(None, "chan", None, "stn", None),
        check_vma=False,
    )
```
